512 devices in a mesh: group: 4 (over y), lat: 16 (over z_hi, x), lon: 8 (over z_lo, core).
Axes of the slice: x: 4, y: 4, z: 16 (z_hi: 4, z_lo: 4; z = z_hi * 4 + z_lo), core: 2. Of those that a mesh axis runs over, the one named last changes fastest.
Arguments:
- species_amounts: float32 [128, 4, 256, 1024], P('group', None, 'lat', 'lon'), may hold values from -4 to 4
- zonal_cell_fraction: float32 [4, 256, 1024], P('group', 'lat', 'lon'), may hold values from -0.3 to 0.3
- meridional_cell_fraction: float32 [4, 256, 1024], P('group', 'lat', 'lon'), may hold values from -0.3 to 0.3
- updraft_cell_fraction: float32 [4, 256, 1024], P('group', 'lat', 'lon'), may hold values from -0.3 to 0.3
- warmth_anomaly: float32 [4, 256, 1024], P('group', 'lat', 'lon'), may hold values from -2 to 2
- mass_per_volume: float32 [4, 256, 1024], P('group', 'lat', 'lon'), may hold values from 0.5 to 2
- chemistry_iterations: int32 [256, 1024], P('lat', 'lon'), may hold values from 1 to 2, as said below
- companion_species: bfloat16 [512, 128], replicated, may hold values from -0.5 to 0.5
- stoichiometric_rate: bfloat16 [128, 512], replicated, may hold values from -0.25 to 0.25
- heat_yield: float32 [128], replicated, may hold values from -0.5 to 0.5
Outputs:
- tracers_out: float32 [128, 4, 256, 1024], P('group', None, 'lat', 'lon')
- east_out: float32 [4, 256, 1024], P('group', 'lat', 'lon')
- north_out: float32 [4, 256, 1024], P('group', 'lat', 'lon')
- temp_out: float32 [4, 256, 1024], P('group', 'lat', 'lon')
The draws below stay inside these ranges and needn't reach their ends.
Inputs may be any that keep to these rules, and one draw needn't show every extreme that they name: `chemistry_iterations`: columns at latitude rows 192 and above hold 1 or 2, and the last row holds 2; all other columns hold 1.
All inputs are finite; a program needn't handle non-finite values.
Results may differ from the reference program's by a relative error of at most 0.0011.
Values sent between devices are 32-bit elements; how exact they have to be, the bound alone decides.
A program may use at most 64 MiB of HBM per device.

```python
import jax
import jax.numpy as jnp
from jax import lax

NTR = 128
NRX = 512
MAXSUB = 2
STEPS = 1
STRATUM_TOTAL = 4
MERIDIAN_SPAN = 256
PARALLEL_SPAN = 1024


def draw_chemistry_iterations(key, part):
    meridian_span = lax.broadcasted_iota(jnp.int32, (MERIDIAN_SPAN, PARALLEL_SPAN), 0)
    jitter = jax.random.randint(key, (MERIDIAN_SPAN, PARALLEL_SPAN), 0, 2).astype(jnp.int32)
    sunlit = meridian_span >= 3 * MERIDIAN_SPAN // 4
    not_last = (meridian_span != MERIDIAN_SPAN - 1).astype(jnp.int32)
    bright = MAXSUB - jitter * not_last
    return jnp.where(sunlit, bright, jnp.ones_like(bright)).astype(jnp.int32)


def levels(key, extent, split, least, largest):
    loudness = 1.0
    for axis_at, blocks in split:
        steps = jax.random.uniform(jax.random.fold_in(jax.random.fold_in(key, 6), axis_at), (blocks,), jnp.float32, least / len(split), largest / len(split))
        loudness = loudness * jnp.repeat(jnp.exp(steps), extent[axis_at] // blocks).reshape((-1,) + (1,) * (len(extent) - 1 - axis_at))
    return loudness


def gaussian(rng, shape, spread, most, cuts=(), dtype=jnp.bfloat16):
    values = spread * jax.random.normal(rng, shape, jnp.float32)
    if cuts:
        values = values * levels(rng, shape, cuts, -0.22, 0.18)
    return jnp.clip(values, -most, most).astype(dtype)


def setup_inputs(seed: int = 0) -> dict:
    key_list = jax.random.split(jax.random.key(seed), 11)
    species_amounts = gaussian(key_list[0], (NTR, STRATUM_TOTAL, MERIDIAN_SPAN, PARALLEL_SPAN), 1.0, 4.0, ((0, 4), (2, 16), (3, 8)), jnp.float32)
    zonal_cell_fraction = jnp.clip(jax.random.uniform(key_list[1], (STRATUM_TOTAL, MERIDIAN_SPAN, PARALLEL_SPAN), jnp.float32, -0.3, 0.3) * levels(key_list[1], (STRATUM_TOTAL, MERIDIAN_SPAN, PARALLEL_SPAN), ((0, 4), (1, 16), (2, 8)), -0.4, 0.0), -0.3, 0.3)
    meridional_cell_fraction = jnp.clip(jax.random.uniform(key_list[2], (STRATUM_TOTAL, MERIDIAN_SPAN, PARALLEL_SPAN), jnp.float32, -0.3, 0.3) * levels(key_list[2], (STRATUM_TOTAL, MERIDIAN_SPAN, PARALLEL_SPAN), ((0, 4), (1, 16), (2, 8)), -0.4, 0.0), -0.3, 0.3)
    updraft_cell_fraction = jnp.clip(jax.random.uniform(key_list[3], (STRATUM_TOTAL, MERIDIAN_SPAN, PARALLEL_SPAN), jnp.float32, -0.3, 0.3) * levels(key_list[3], (STRATUM_TOTAL, MERIDIAN_SPAN, PARALLEL_SPAN), ((0, 4), (1, 16), (2, 8)), -0.4, 0.0), -0.3, 0.3)
    warmth_anomaly = gaussian(key_list[4], (STRATUM_TOTAL, MERIDIAN_SPAN, PARALLEL_SPAN), 0.5, 2.0, ((0, 4), (1, 16), (2, 8)), jnp.float32)
    mass_per_volume = jnp.clip(0.5 + 1.5 * jax.random.uniform(key_list[5], (STRATUM_TOTAL, MERIDIAN_SPAN, PARALLEL_SPAN), jnp.float32) ** levels(key_list[5], (STRATUM_TOTAL, MERIDIAN_SPAN, PARALLEL_SPAN), ((0, 4), (1, 16), (2, 8)), -0.2, 0.2), 0.5, 2.0)
    chemistry_iterations = draw_chemistry_iterations(jax.random.fold_in(key_list[10], 71), 0)
    companion_species = gaussian(key_list[7], (NRX, NTR), NTR ** -0.5, 0.5)
    stoichiometric_rate = gaussian(key_list[8], (NTR, NRX), NRX ** -0.5, 0.25)
    heat_yield = gaussian(key_list[9], (NTR,), NTR ** -0.5, 0.5, (), jnp.float32)
    return dict(species_amounts=species_amounts, zonal_cell_fraction=zonal_cell_fraction, meridional_cell_fraction=meridional_cell_fraction, updraft_cell_fraction=updraft_cell_fraction, warmth_anomaly=warmth_anomaly, mass_per_volume=mass_per_volume, chemistry_iterations=chemistry_iterations, companion_species=companion_species, stoichiometric_rate=stoichiometric_rate, heat_yield=heat_yield)


diffusion = 0.1
pressure = 0.05
chem_step = 0.2
block_cells = 512


def transport(padded, east_pad, north_pad, upward):
    zonal_cells = padded[..., 1:-1, :]
    zonal_wind = east_pad[:, 1:-1, :]
    face_wind = 0.5 * (zonal_wind[..., :-1] + zonal_wind[..., 1:])
    face_flux = jnp.maximum(face_wind, 0.0) * zonal_cells[..., :-1] + jnp.minimum(face_wind, 0.0) * zonal_cells[..., 1:]
    change = face_flux[..., 1:] - face_flux[..., :-1]
    north_cells = padded[..., 1:-1]
    north_wind = north_pad[:, :, 1:-1]
    face_wind = 0.5 * (north_wind[:, :-1] + north_wind[:, 1:])
    face_flux = jnp.maximum(face_wind, 0.0) * north_cells[..., :-1, :] + jnp.minimum(face_wind, 0.0) * north_cells[..., 1:, :]
    change = change + (face_flux[..., 1:, :] - face_flux[..., :-1, :])
    centre = padded[..., 1:-1, 1:-1]
    face_wind = 0.5 * (upward[:-1] + upward[1:])
    face_flux = jnp.maximum(face_wind, 0.0) * centre[..., :-1, :, :] + jnp.minimum(face_wind, 0.0) * centre[..., 1:, :, :]
    closed = jnp.zeros_like(face_flux[..., :1, :, :])
    face_flux = jnp.concatenate([closed, face_flux, closed], axis=-3)
    change = change + (face_flux[..., 1:, :, :] - face_flux[..., :-1, :, :])
    return centre - change


def dynamics(padded):
    centre = padded[:, :, 1:-1, 1:-1]
    eastern = padded[:, :, 1:-1, 2:]
    western = padded[:, :, 1:-1, :-2]
    northern = padded[:, :, 2:, 1:-1]
    southern = padded[:, :, :-2, 1:-1]
    laplace = eastern + western + northern + southern - 4.0 * centre
    diffused = centre + diffusion * laplace
    zonal_axis_name = diffused[0] - pressure * (eastern[2] - western[2])
    meridional_axis_name = diffused[1] - pressure * (northern[2] - southern[2])
    return zonal_axis_name, meridional_axis_name, diffused[2]


def react_block(tracer_block, rate_block, count_block, companion_species, stoichiometric_rate, heat_yield):
    species = tracer_block.shape[0]
    width = tracer_block.shape[1]
    repeats = companion_species.shape[0] // species
    deepest = jnp.max(count_block)

    def keep_going(state_pair):
        return state_pair[0] < deepest

    def substep(state_pair):
        counter, current = state_pair
        narrow = current.astype(jnp.bfloat16)
        pair_terms = jnp.dot(companion_species, narrow, preferred_element_type=jnp.float32)
        quadratic = (pair_terms.reshape(repeats, species, width) * current[None]).reshape(repeats * species, width).astype(jnp.bfloat16)
        tendency = rate_block[None] * jnp.dot(stoichiometric_rate, quadratic, preferred_element_type=jnp.float32) - current
        current = jnp.where(counter < count_block[None], current + chem_step * tendency, current)
        return counter + 1, current

    final = lax.while_loop(keep_going, substep, (jnp.zeros((), jnp.int32), tracer_block))[1]
    heating = jnp.dot(heat_yield[None], final - tracer_block, precision=lax.Precision.HIGHEST)[0]
    return final, heating


def reference(species_amounts, zonal_cell_fraction, meridional_cell_fraction, updraft_cell_fraction, warmth_anomaly, mass_per_volume, chemistry_iterations, companion_species, stoichiometric_rate, heat_yield):
    species = species_amounts.shape[0]
    stratum_total, meridian_span, parallel_span = warmth_anomaly.shape
    cell_count = stratum_total * meridian_span * parallel_span
    block_count = cell_count // block_cells
    counts = jnp.broadcast_to(chemistry_iterations[None], (stratum_total, meridian_span, parallel_span)).reshape(block_count, block_cells).astype(jnp.int32)
    zonal_axis_name, meridional_axis_name, heat_snapshot = zonal_cell_fraction, meridional_cell_fraction, warmth_anomaly
    concentration = species_amounts
    for coupling in range(STEPS):
        fields = jnp.stack([zonal_axis_name, meridional_axis_name, heat_snapshot])
        padded_fields = jnp.pad(fields, ((0, 0), (0, 0), (1, 1), (1, 1)))
        padded_tracers = jnp.pad(concentration, ((0, 0), (0, 0), (1, 1), (1, 1)))
        advected = transport(padded_tracers, padded_fields[0], padded_fields[1], updraft_cell_fraction)
        new_east, new_north, warmed = dynamics(padded_fields)
        reaction_rate = jax.nn.sigmoid(2.0 * heat_snapshot).reshape(block_count, block_cells)
        blocks = advected.reshape(species, block_count, block_cells).transpose(1, 0, 2)

        def one_block(pieces):
            return react_block(pieces[0], pieces[1], pieces[2], companion_species, stoichiometric_rate, heat_yield)

        reacted, heating = lax.map(one_block, (blocks, reaction_rate, counts))
        concentration = reacted.transpose(1, 0, 2).reshape(concentration.shape)
        heat_snapshot = warmed + heating.reshape(stratum_total, meridian_span, parallel_span) / mass_per_volume
        zonal_axis_name, meridional_axis_name = new_east, new_north
    return concentration, zonal_axis_name, meridional_axis_name, heat_snapshot
```

```python
import functools

import jax
import jax.numpy as jnp
from jax import lax
from jax.experimental import pallas as pl
from jax.experimental.pallas import tpu as pltpu
from jax.sharding import PartitionSpec as P

MESH = pl.DeviceIdType.MESH
diffusion = 0.1
pressure = 0.05
chem_step = 0.2


def kernel(
    sizes,
    species,
    east,
    north,
    up,
    warm,
    dens,
    counts,
    comp,
    stoi,
    heat,
    back,
    small,
    raw,
    cells,
    packs,
    sides,
    adv,
    block,
    reacted,
    own,
    winds,
    side_u,
    side_vt,
    rim_out,
    rim_in,
    coef,
    misc,
    count_v,
    comp_v,
    stoi_v,
    heat_v,
    heat_b,
    small_v,
    load_sem,
    wind_sem,
    lat_sem,
    rim_sem,
    lon_sem,
    lonu_sem,
    lonv_sem,
    fwd_sem,
    back_sem,
    local_sem,
    out_sem,
):
    groups, lats, lons = sizes
    g, la, lo = lax.axis_index("group"), lax.axis_index("lat"), lax.axis_index("lon")
    levels, rows, own_tr, width = adv.shape
    species_all = comp_v.shape[1]
    repeats = comp_v.shape[0] // species_all
    pieces = rows // 2
    peers = [lax.rem(g + k, groups) for k in range(1, groups)]
    has_s, has_n, has_w, has_e = la > 0, la < lats - 1, lo > 0, lo < lons - 1
    dev_s, dev_n, dev_w, dev_e = (g, la - 1, lo), (g, la + 1, lo), (g, la, lo - 1), (g, la, lo + 1)

    barrier = pltpu.get_barrier_semaphore()

    def greet(dev):
        pl.semaphore_signal(barrier, inc=1, device_id=dev, device_id_type=MESH)

    for p in peers:
        greet((p, la, lo))
    for has, dev in ((has_s, dev_s), (has_n, dev_n), (has_w, dev_w), (has_e, dev_e)):
        pl.when(has)(functools.partial(greet, dev))

    part = own_tr * levels * rows // 4
    loads = [
        pltpu.make_async_copy(src, dst, load_sem.at[i])
        for i, (src, dst) in enumerate(
            [
                (species.at[pl.ds(n * part, part)], raw.at[pl.ds(n * part, part)])
                for n in range(4)
            ]
            + [
                (up.at[0], own.at[0]),
                (east.at[0], own.at[1]),
                (north.at[0], own.at[2]),
                (warm.at[0], own.at[3]),
                (dens.at[0], misc.at[0]),
                (counts, count_v),
                (comp, comp_v),
                (stoi, stoi_v),
                (heat, heat_v),
            ]
        )
    ]
    for i in list(range(4, 8)) + list(range(4)) + list(range(8, 13)):
        loads[i].start()

    @pl.when(jnp.logical_not(has_s))
    def _():
        cells[:, 0] = jnp.zeros((levels, own_tr, width), jnp.float32)
        rim_in[0] = jnp.zeros((8, width), jnp.float32)

    @pl.when(jnp.logical_not(has_n))
    def _():
        cells[:, rows + 1] = jnp.zeros((levels, own_tr, width), jnp.float32)
        rim_in[1] = jnp.zeros((8, width), jnp.float32)

    @pl.when(jnp.logical_not(has_w))
    def _():
        sides[0] = jnp.zeros((own_tr, width), jnp.float32)
        side_u[0] = jnp.zeros((levels, rows, width), jnp.float32)
        side_vt[0] = jnp.zeros((2, rows, width), jnp.float32)

    @pl.when(jnp.logical_not(has_e))
    def _():
        sides[1] = jnp.zeros((own_tr, width), jnp.float32)
        side_u[1] = jnp.zeros((levels, rows, width), jnp.float32)
        side_vt[1] = jnp.zeros((2, rows, width), jnp.float32)

    lane = lax.broadcasted_iota(jnp.int32, (own_tr, width), 1)

    for i in range(4):
        loads[i].wait()

    def turn(r, packed):
        west, eastern = packed
        for l in range(levels):
            q = l * rows + r
            tile = raw[pl.ds(q, own_tr, stride=levels * rows), :]
            cells[l, r + 1] = tile
            hit = lane == q
            west = jnp.where(hit, pltpu.roll(tile, q, 1), west)
            eastern = jnp.where(hit, pltpu.roll(tile, q + 1, 1), eastern)
        return west, eastern

    zero = jnp.zeros((own_tr, width), jnp.float32)
    west, eastern = lax.fori_loop(0, rows, turn, (zero, zero))
    packs[0] = eastern
    packs[1] = west
    for i in range(4, 8):
        loads[i].wait()
    winds[g] = own[0:3]

    n_greet = (
        groups
        - 1
        + has_s.astype(jnp.int32)
        + has_n.astype(jnp.int32)
        + has_w.astype(jnp.int32)
        + has_e.astype(jnp.int32)
    )
    pl.semaphore_wait(barrier, n_greet)

    def remote(src, dst, sems, index, dev):
        return pltpu.make_async_remote_copy(
            src_ref=src,
            dst_ref=dst,
            send_sem=sems.at[(0,) + index],
            recv_sem=sems.at[(1,) + index],
            device_id=dev,
            device_id_type=MESH,
        )

    def wind_copy(k, level):
        return remote(own.at[pl.ds(0, 3)], winds.at[level], wind_sem, (k,), (peers[k], la, lo))

    for k in range(groups - 1):
        wind_copy(k, g).start()
    lon_copies = [
        (has_e, has_w, remote(packs.at[0], sides.at[0], lon_sem, (0,), dev_e)),
        (has_w, has_e, remote(packs.at[1], sides.at[1], lon_sem, (1,), dev_w)),
    ]
    lat_copies = [
        (has_n, has_s, remote(cells.at[:, rows], cells.at[:, 0], lat_sem, (0,), dev_n)),
        (has_s, has_n, remote(cells.at[:, 1], cells.at[:, rows + 1], lat_sem, (1,), dev_s)),
    ]
    lonv_copies = [
        (has_e, has_w, remote(own.at[pl.ds(2, 2)], side_vt.at[0], lonv_sem, (0,), dev_e)),
        (has_w, has_e, remote(own.at[pl.ds(2, 2)], side_vt.at[1], lonv_sem, (1,), dev_w)),
    ]
    wind_u = winds.at[:, 1]
    lonu_copies = [
        (has_e, has_w, remote(wind_u, side_u.at[0], lonu_sem, (0,), dev_e)),
        (has_w, has_e, remote(wind_u, side_u.at[1], lonu_sem, (1,), dev_w)),
    ]
    rim_copies = [
        (has_n, has_s, remote(rim_out.at[0], rim_in.at[0], rim_sem, (0,), dev_n)),
        (has_s, has_n, remote(rim_out.at[1], rim_in.at[1], rim_sem, (1,), dev_s)),
    ]

    def start_all(copies):
        for sends, _, copy in copies:
            pl.when(sends)(copy.start)

    def receive_all(copies):
        for _, receives, copy in copies:
            pl.when(receives)(copy.wait_recv)

    start_all(lon_copies)
    start_all(lat_copies)

    for k in range(groups - 1):
        wind_copy(k, lax.rem(g + groups - 1 - k, groups)).wait_recv()
    start_all(lonu_copies)
    for l in range(levels):
        rim_out[0, l : l + 1, :] = winds[l, 2, rows - 1 : rows, :]
        rim_out[1, l : l + 1, :] = winds[l, 2, 0:1, :]
    for j in range(3):
        rim_out[0, levels + j : levels + j + 1, :] = own[1 + j, rows - 1 : rows, :]
        rim_out[1, levels + j : levels + j + 1, :] = own[1 + j, 0:1, :]
    start_all(rim_copies)
    start_all(lonv_copies)

    row_at = lax.broadcasted_iota(jnp.int32, (rows, width), 0)
    lane_at = lax.broadcasted_iota(jnp.int32, (rows, width), 1)

    def from_west(f, edge):
        return jnp.where(lane_at == 0, pltpu.roll(edge, 1, 1), pltpu.roll(f, 1, 1))

    def from_east(f, edge):
        return jnp.where(
            lane_at == width - 1, pltpu.roll(edge, width - 1, 1), pltpu.roll(f, width - 1, 1)
        )

    def from_south(f, edge):
        return jnp.where(row_at == 0, edge, pltpu.roll(f, 1, 0))

    def from_north(f, edge):
        return jnp.where(row_at == rows - 1, edge, pltpu.roll(f, rows - 1, 0))

    def zonal_vertical():
        for l in range(levels):
            u = winds[l, 1]
            a_e = 0.5 * (u + from_east(u, side_u[1, l]))
            a_w = 0.5 * (from_west(u, side_u[0, l]) + u)
            keep = 1.0 - jnp.maximum(a_e, 0.0) + jnp.minimum(a_w, 0.0)
            coef[1, l] = -jnp.minimum(a_e, 0.0)
            coef[2, l] = jnp.maximum(a_w, 0.0)
            if l < levels - 1:
                a_u = 0.5 * (winds[l, 0] + winds[l + 1, 0])
                keep = keep - jnp.maximum(a_u, 0.0)
                coef[5, l] = -jnp.minimum(a_u, 0.0)
            if l > 0:
                a_d = 0.5 * (winds[l - 1, 0] + winds[l, 0])
                keep = keep + jnp.minimum(a_d, 0.0)
                coef[6, l] = jnp.maximum(a_d, 0.0)
            coef[7, l] = keep

    def meridional(south_rim, north_rim):
        for l in range(levels):
            v = winds[l, 2]
            a_n = 0.5 * (v + from_north(v, north_rim(l)))
            a_s = 0.5 * (from_south(v, south_rim(l)) + v)
            coef[3, l] = -jnp.minimum(a_n, 0.0)
            coef[4, l] = jnp.maximum(a_s, 0.0)
            coef[0, l] = coef[7, l] - jnp.maximum(a_n, 0.0) + jnp.minimum(a_s, 0.0)

    receive_all(lonu_copies)
    zonal_vertical()
    meridional(lambda l: winds[l, 2, 0:1, :], lambda l: winds[l, 2, 0:1, :])
    receive_all(lon_copies)

    def first_row(i):
        odd = i % 2
        half = i // 2
        middle = pieces // 2
        return 2 * (odd * (middle + half) + (1 - odd) * (middle - 1 - half))

    mine = pl.ds(pl.multiple_of(g * own_tr, own_tr), own_tr)

    def forward_copy(i, k, part):
        r0 = first_row(i)
        part = pl.ds(pl.multiple_of(part * own_tr, own_tr), own_tr)
        return remote(
            adv.at[peers[k], pl.ds(r0, 2)],
            block.at[pl.ds(r0, 2), part],
            fwd_sem,
            (i, k),
            (peers[k], la, lo),
        )

    def advect(i, carry):
        r0 = first_row(i)
        for rr in range(2):
            r = r0 + rr
            for l in range(levels):
                q = l * rows + r

                def c(j):
                    return coef[j, l, pl.ds(r, 1), :]

                here = cells[l, r + 1]
                east_of = jnp.where(
                    lane == width - 1,
                    pltpu.roll(sides[1], width - 1 - q, 1),
                    pltpu.roll(here, width - 1, 1),
                )
                west_of = jnp.where(
                    lane == 0,
                    pltpu.roll(sides[0], lax.rem(width - q, width), 1),
                    pltpu.roll(here, 1, 1),
                )
                total = c(0) * here + c(1) * east_of + c(2) * west_of
                total = total + c(3) * cells[l, r + 2] + c(4) * cells[l, r]
                if l < levels - 1:
                    total = total + c(5) * cells[l + 1, r + 1]
                if l > 0:
                    total = total + c(6) * cells[l - 1, r + 1]
                adv[l, r] = total
            block[r, mine, :] = adv[g, r]
        for k in range(groups - 1):
            forward_copy(i, k, g).start()
        return carry

    lax.fori_loop(0, pieces - 2, advect, 0)

    receive_all(rim_copies)
    receive_all(lat_copies)
    meridional(lambda l: rim_in[0, l : l + 1, :], lambda l: rim_in[1, l : l + 1, :])
    lax.fori_loop(pieces - 2, pieces, advect, 0)

    for i in range(8, 13):
        loads[i].wait()
    receive_all(lonv_copies)
    t = own[3]
    misc[1] = 1.0 / (1.0 + jnp.exp(-2.0 * t))
    heat_b[...] = jnp.transpose(jnp.broadcast_to(heat_v[...], (species_all, species_all)))

    def around(f, j, west_tile, east_tile):
        s, n = rim_in[0, levels + j : levels + j + 1, :], rim_in[1, levels + j : levels + j + 1, :]
        return from_east(f, east_tile), from_west(f, west_tile), from_north(f, n), from_south(f, s)

    t_e, t_w, t_n, t_s = around(t, 2, side_vt[0, 1], side_vt[1, 1])
    u = own[1]
    e, w, n, s = around(u, 0, side_u[0, g], side_u[1, g])
    small_v[0] = u + diffusion * (e + w + n + s - 4.0 * u) - pressure * (t_e - t_w)
    v = own[2]
    e, w, n, s = around(v, 1, side_vt[0, 0], side_vt[1, 0])
    small_v[1] = v + diffusion * (e + w + n + s - 4.0 * v) - pressure * (t_n - t_s)
    misc[2] = t + diffusion * (t_e + t_w + t_n + t_s - 4.0 * t)

    def back_copy(i, k, level):
        r0 = first_row(i)
        part = pl.ds(pl.multiple_of(peers[k] * own_tr, own_tr), own_tr)
        return remote(
            reacted.at[pl.ds(r0, 2), part],
            back.at[level, pl.ds(r0, 2)],
            back_sem,
            (i, k),
            (peers[k], la, lo),
        )

    def local_copy(i):
        r0 = first_row(i)
        return pltpu.make_async_copy(
            reacted.at[pl.ds(r0, 2), mine], back.at[g, pl.ds(r0, 2)], local_sem.at[i]
        )

    twice = (la + 1) * rows > 3 * lats * rows // 4

    def react(i, carry):
        r0 = first_row(i)
        for k in range(groups - 1):
            forward_copy(i, k, lax.rem(g + groups - 1 - k, groups)).wait_recv()

        def pair_of(ref):
            return jnp.concatenate([ref[pl.ds(r0, 1), :], ref[pl.ds(r0 + 1, 1), :]], axis=1)

        rate = pair_of(misc.at[1])
        count = pair_of(count_v)

        def substep(current, counter):
            narrow = current.astype(jnp.bfloat16)
            pair_terms = jnp.dot(comp_v[...], narrow, preferred_element_type=jnp.float32)
            quad = (
                (pair_terms.reshape(repeats, species_all, 2 * width) * current[None])
                .reshape(repeats * species_all, 2 * width)
                .astype(jnp.bfloat16)
            )
            made = jnp.dot(stoi_v[...], quad, preferred_element_type=jnp.float32)
            later = current + chem_step * (rate * made - current)
            return jnp.where(counter < count, later, current)

        def load(ref):
            return jnp.concatenate([ref[r0], ref[r0 + 1]], axis=1)

        def keep(value):
            reacted[r0] = value[:, :width]
            reacted[r0 + 1] = value[:, width:]

        keep(substep(load(block), 0))

        @pl.when(twice)
        def _():
            keep(substep(load(reacted), 1))

        for k in range(groups - 1):
            back_copy(i, k, g).start()
        local_copy(i).start()
        for rr in range(2):
            r = r0 + rr
            gain = heat_b[...] * (reacted[r] - block[r])
            misc[3, pl.ds(r, 1), :] = jnp.sum(gain, axis=0, keepdims=True)
        return carry

    lax.fori_loop(0, pieces, react, 0)

    small_v[2] = misc[2] + misc[3] / misc[0]
    out = pltpu.make_async_copy(small_v, small, out_sem)
    out.start()

    for sends, _, copy in lon_copies + lat_copies + lonv_copies + lonu_copies + rim_copies:
        pl.when(sends)(copy.wait_send)
    for k in range(groups - 1):
        wind_copy(k, g).wait_send()

    def finish(i, carry):
        for k in range(groups - 1):
            forward_copy(i, k, g).wait_send()
            back_copy(i, k, g).wait_send()
            back_copy(i, k, lax.rem(g + groups - 1 - k, groups)).wait_recv()
        local_copy(i).wait()
        return carry

    lax.fori_loop(0, pieces, finish, 0)
    out.wait()


def unload(back, small, tracers, east, north, temp):
    levels, rows, some, width = back.shape
    for t in range(some):
        for l in range(levels):
            for r in range(0, rows, 8):
                tracers[t, l, r : r + 8, :] = back[l, r : r + 8, t, :]

    @pl.when(pl.program_id(0) == 0)
    def _():
        east[0] = small[0]
        north[0] = small[1]
        temp[0] = small[2]


def local(sizes, species, east, north, up, warm, dens, counts, comp, stoi, heat):
    own_tr, levels, rows, width = species.shape
    all_tr, terms = stoi.shape
    groups = sizes[0]
    pieces = rows // 2
    f32 = jnp.float32
    dma = pltpu.SemaphoreType.DMA
    back, small = pl.pallas_call(
        functools.partial(kernel, sizes),
        out_shape=(
            jax.ShapeDtypeStruct((levels, rows, own_tr, width), f32),
            jax.ShapeDtypeStruct((3, rows, width), f32),
        ),
        in_specs=[pl.BlockSpec(memory_space=pltpu.HBM)] * 10,
        out_specs=[pl.BlockSpec(memory_space=pltpu.HBM)] * 2,
        scratch_shapes=[
            pltpu.VMEM((own_tr * levels * rows, width), f32),
            pltpu.VMEM((levels, rows + 2, own_tr, width), f32),
            pltpu.VMEM((2, own_tr, width), f32),
            pltpu.VMEM((2, own_tr, width), f32),
            pltpu.VMEM((levels, rows, own_tr, width), f32),
            pltpu.VMEM((rows, all_tr, width), f32),
            pltpu.VMEM((rows, all_tr, width), f32),
            pltpu.VMEM((4, rows, width), f32),
            pltpu.VMEM((levels, 3, rows, width), f32),
            pltpu.VMEM((2, levels, rows, width), f32),
            pltpu.VMEM((2, 2, rows, width), f32),
            pltpu.VMEM((2, 8, width), f32),
            pltpu.VMEM((2, 8, width), f32),
            pltpu.VMEM((8, levels, rows, width), f32),
            pltpu.VMEM((4, rows, width), f32),
            pltpu.VMEM((rows, width), jnp.int32),
            pltpu.VMEM((terms, all_tr), jnp.bfloat16),
            pltpu.VMEM((all_tr, terms), jnp.bfloat16),
            pltpu.VMEM((1, all_tr), f32),
            pltpu.VMEM((all_tr, all_tr), f32),
            pltpu.VMEM((3, rows, width), f32),
            dma((13,)),
            dma((2, groups - 1)),
            dma((2, 2)),
            dma((2, 2)),
            dma((2, 2)),
            dma((2, 2)),
            dma((2, 2)),
            dma((2, pieces, groups - 1)),
            dma((2, pieces, groups - 1)),
            dma((pieces,)),
            dma(()),
        ],
        compiler_params=pltpu.CompilerParams(
            collective_id=0, has_side_effects=True, vmem_limit_bytes=63 << 20
        ),
        name="couple",
    )(
        species.reshape(own_tr * levels * rows, width),
        east,
        north,
        up,
        warm,
        dens,
        counts,
        comp,
        stoi,
        heat.reshape(1, all_tr),
    )
    some = 8
    field = pl.BlockSpec((1, rows, width), lambda i: (0, 0, 0))
    return pl.pallas_call(
        unload,
        grid=(own_tr // some,),
        out_shape=(jax.ShapeDtypeStruct((own_tr, levels, rows, width), f32),)
        + (jax.ShapeDtypeStruct((1, rows, width), f32),) * 3,
        in_specs=[
            pl.BlockSpec((levels, rows, some, width), lambda i: (0, 0, i, 0)),
            pl.BlockSpec((3, rows, width), lambda i: (0, 0, 0)),
        ],
        out_specs=[
            pl.BlockSpec((some, levels, rows, width), lambda i: (i, 0, 0, 0)),
            field,
            field,
            field,
        ],
        name="unload",
    )(back, small)


def solution(mesh):
    sizes = (mesh.shape["group"], mesh.shape["lat"], mesh.shape["lon"])
    fields = P("group", "lat", "lon")
    return jax.shard_map(
        functools.partial(local, sizes),
        mesh=mesh,
        in_specs=(
            P("group", None, "lat", "lon"),
            fields,
            fields,
            fields,
            fields,
            fields,
            P("lat", "lon"),
            P(),
            P(),
            P(),
        ),
        out_specs=(P("group", None, "lat", "lon"), fields, fields, fields),
        check_vma=False,
    )
```

```python
import functools

import jax
import jax.numpy as jnp
from jax import lax
from jax.experimental import pallas as pl
from jax.experimental.pallas import tpu as pltpu
from jax.sharding import PartitionSpec as P

MESH = pl.DeviceIdType.MESH
diffusion = 0.1
pressure = 0.05
chem_step = 0.2


def kernel(
    sizes,
    species,
    east,
    north,
    up,
    warm,
    dens,
    counts,
    comp,
    stoi,
    heat,
    tracers,
    east_out,
    north_out,
    temp_out,
    raw,
    cells,
    packs,
    sides,
    adv,
    block,
    reacted,
    back,
    own,
    winds,
    side_u,
    side_vt,
    rim_out,
    rim_in,
    coef,
    misc,
    count_v,
    comp_v,
    stoi_v,
    heat_v,
    heat_b,
    load_sem,
    wind_sem,
    lat_sem,
    rim_sem,
    lon_sem,
    lonu_sem,
    lonv_sem,
    fwd_sem,
    back_sem,
    ok_sem,
):
    groups, lats, lons = sizes
    g, la, lo = lax.axis_index("group"), lax.axis_index("lat"), lax.axis_index("lon")
    levels, rows, own_tr, width = adv.shape
    species_all = comp_v.shape[1]
    repeats = comp_v.shape[0] // species_all
    pieces = rows // 2
    peers = [lax.rem(g + k, groups) for k in range(1, groups)]
    has_s, has_n, has_w, has_e = la > 0, la < lats - 1, lo > 0, lo < lons - 1
    dev_s, dev_n, dev_w, dev_e = (g, la - 1, lo), (g, la + 1, lo), (g, la, lo - 1), (g, la, lo + 1)

    turned = la == 3 * lats // 4
    odd = lax.rem(lo, 2) == 1
    near = [
        (has_s, dev_s, turned),
        (has_n, dev_n, la != 3 * lats // 4 - 1),
        (has_w, dev_w, odd),
        (has_e, dev_e, odd),
    ]
    leads = [jnp.logical_and(has, lead) for has, _, lead in near]
    follows = [jnp.logical_and(has, jnp.logical_not(lead)) for has, _, lead in near]
    barrier = pltpu.get_barrier_semaphore()

    def greet(dev):
        pl.semaphore_signal(barrier, inc=1, device_id=dev, device_id_type=MESH)

    for p in peers:
        greet((p, la, lo))
    for lead, (_, dev, _) in zip(leads, near):
        pl.when(lead)(functools.partial(greet, dev))

    def answer(i):
        pl.semaphore_signal(
            ok_sem.at[i ^ 1], inc=1, device_id=near[i][1], device_id_type=MESH
        )

    def await_answer(i):
        pl.when(leads[i])(lambda: pl.semaphore_wait(ok_sem.at[i], 1))

    part = own_tr * levels * rows // 4
    loads = [
        pltpu.make_async_copy(src, dst, load_sem.at[i])
        for i, (src, dst) in enumerate(
            [
                (species.at[pl.ds(n * part, part)], raw.at[pl.ds(n * part, part)])
                for n in range(4)
            ]
            + [
                (up.at[0], own.at[0]),
                (east.at[0], own.at[1]),
                (north.at[0], own.at[2]),
                (warm.at[0], own.at[3]),
                (dens.at[0], misc.at[0]),
                (counts, count_v),
                (comp, comp_v),
                (stoi, stoi_v),
                (heat, heat_v),
            ]
        )
    ]
    for i in list(range(4, 8)) + list(range(4)) + list(range(8, 13)):
        loads[i].start()

    @pl.when(jnp.logical_not(has_s))
    def _():
        cells[:, 0] = jnp.zeros((levels, own_tr, width), jnp.float32)
        rim_in[0] = jnp.zeros((8, width), jnp.float32)

    @pl.when(jnp.logical_not(has_n))
    def _():
        cells[:, rows + 1] = jnp.zeros((levels, own_tr, width), jnp.float32)
        rim_in[1] = jnp.zeros((8, width), jnp.float32)

    @pl.when(jnp.logical_not(has_w))
    def _():
        sides[0] = jnp.zeros((own_tr, width), jnp.float32)
        side_u[0] = jnp.zeros((levels, rows, width), jnp.float32)
        side_vt[0] = jnp.zeros((2, rows, width), jnp.float32)

    @pl.when(jnp.logical_not(has_e))
    def _():
        sides[1] = jnp.zeros((own_tr, width), jnp.float32)
        side_u[1] = jnp.zeros((levels, rows, width), jnp.float32)
        side_vt[1] = jnp.zeros((2, rows, width), jnp.float32)

    for i in range(4, 8):
        loads[i].wait()
    winds[g] = own[0:3]

    pl.semaphore_wait(barrier, groups - 1 + sum(f.astype(jnp.int32) for f in follows))
    for i in range(4):
        pl.when(follows[i])(functools.partial(answer, i))

    def remote(src, dst, sems, index, dev):
        return pltpu.make_async_remote_copy(
            src_ref=src,
            dst_ref=dst,
            send_sem=sems.at[(0,) + index],
            recv_sem=sems.at[(1,) + index],
            device_id=dev,
            device_id_type=MESH,
        )

    def wind_copy(k, level):
        return remote(own.at[pl.ds(0, 3)], winds.at[level], wind_sem, (k,), (peers[k], la, lo))

    for k in range(groups - 1):
        wind_copy(k, g).start()

    lane = lax.broadcasted_iota(jnp.int32, (own_tr, width), 1)

    for i in range(4):
        loads[i].wait()

    def turn(r, packed):
        west, eastern = packed
        for l in range(levels):
            q = l * rows + r
            tile = raw[pl.ds(q, own_tr, stride=levels * rows), :]
            cells[l, r + 1] = tile
            hit = lane == q
            west = jnp.where(hit, pltpu.roll(tile, q, 1), west)
            eastern = jnp.where(hit, pltpu.roll(tile, q + 1, 1), eastern)
        return west, eastern

    zero = jnp.zeros((own_tr, width), jnp.float32)
    west, eastern = lax.fori_loop(0, rows, turn, (zero, zero))
    packs[0] = eastern
    packs[1] = west
    lon_copies = [
        (has_e, has_w, remote(packs.at[0], sides.at[0], lon_sem, (0,), dev_e)),
        (has_w, has_e, remote(packs.at[1], sides.at[1], lon_sem, (1,), dev_w)),
    ]
    lat_copies = [
        (has_n, has_s, remote(cells.at[:, rows], cells.at[:, 0], lat_sem, (0,), dev_n)),
        (has_s, has_n, remote(cells.at[:, 1], cells.at[:, rows + 1], lat_sem, (1,), dev_s)),
    ]
    lonv_copies = [
        (has_e, has_w, remote(own.at[pl.ds(2, 2)], side_vt.at[0], lonv_sem, (0,), dev_e)),
        (has_w, has_e, remote(own.at[pl.ds(2, 2)], side_vt.at[1], lonv_sem, (1,), dev_w)),
    ]
    wind_u = winds.at[:, 1]
    lonu_copies = [
        (has_e, has_w, remote(wind_u, side_u.at[0], lonu_sem, (0,), dev_e)),
        (has_w, has_e, remote(wind_u, side_u.at[1], lonu_sem, (1,), dev_w)),
    ]
    rim_copies = [
        (has_n, has_s, remote(rim_out.at[0], rim_in.at[0], rim_sem, (0,), dev_n)),
        (has_s, has_n, remote(rim_out.at[1], rim_in.at[1], rim_sem, (1,), dev_s)),
    ]

    def start_all(copies):
        for sends, _, copy in copies:
            pl.when(sends)(copy.start)

    def receive_all(copies):
        for _, receives, copy in copies:
            pl.when(receives)(copy.wait_recv)

    def start_lat(copies, which):
        pl.when(which[1])(copies[0][2].start)
        pl.when(which[0])(copies[1][2].start)

    start_lat(lat_copies, follows)
    await_answer(3)
    pl.when(has_e)(lon_copies[0][2].start)
    await_answer(2)
    pl.when(has_w)(lon_copies[1][2].start)

    for k in range(groups - 1):
        wind_copy(k, lax.rem(g + groups - 1 - k, groups)).wait_recv()
    start_all(lonu_copies)
    for l in range(levels):
        rim_out[0, l : l + 1, :] = winds[l, 2, rows - 1 : rows, :]
        rim_out[1, l : l + 1, :] = winds[l, 2, 0:1, :]
    for j in range(3):
        rim_out[0, levels + j : levels + j + 1, :] = own[1 + j, rows - 1 : rows, :]
        rim_out[1, levels + j : levels + j + 1, :] = own[1 + j, 0:1, :]
    start_lat(rim_copies, follows)
    start_all(lonv_copies)

    row_at = lax.broadcasted_iota(jnp.int32, (rows, width), 0)
    lane_at = lax.broadcasted_iota(jnp.int32, (rows, width), 1)

    def from_west(f, edge):
        return jnp.where(lane_at == 0, pltpu.roll(edge, 1, 1), pltpu.roll(f, 1, 1))

    def from_east(f, edge):
        return jnp.where(
            lane_at == width - 1, pltpu.roll(edge, width - 1, 1), pltpu.roll(f, width - 1, 1)
        )

    def from_south(f, edge):
        return jnp.where(row_at == 0, edge, pltpu.roll(f, 1, 0))

    def from_north(f, edge):
        return jnp.where(row_at == rows - 1, edge, pltpu.roll(f, rows - 1, 0))

    def zonal_vertical():
        for l in range(levels):
            u = winds[l, 1]
            a_e = 0.5 * (u + from_east(u, side_u[1, l]))
            a_w = 0.5 * (from_west(u, side_u[0, l]) + u)
            keep = 1.0 - jnp.maximum(a_e, 0.0) + jnp.minimum(a_w, 0.0)
            coef[1, l] = -jnp.minimum(a_e, 0.0)
            coef[2, l] = jnp.maximum(a_w, 0.0)
            if l < levels - 1:
                a_u = 0.5 * (winds[l, 0] + winds[l + 1, 0])
                keep = keep - jnp.maximum(a_u, 0.0)
                coef[5, l] = -jnp.minimum(a_u, 0.0)
            if l > 0:
                a_d = 0.5 * (winds[l - 1, 0] + winds[l, 0])
                keep = keep + jnp.minimum(a_d, 0.0)
                coef[6, l] = jnp.maximum(a_d, 0.0)
            coef[7, l] = keep

    def meridional(south_rim, north_rim):
        for l in range(levels):
            v = winds[l, 2]
            a_n = 0.5 * (v + from_north(v, north_rim(l)))
            a_s = 0.5 * (from_south(v, south_rim(l)) + v)
            coef[3, l] = -jnp.minimum(a_n, 0.0)
            coef[4, l] = jnp.maximum(a_s, 0.0)
            coef[0, l] = coef[7, l] - jnp.maximum(a_n, 0.0) + jnp.minimum(a_s, 0.0)

    receive_all(lonu_copies)
    zonal_vertical()
    meridional(lambda l: winds[l, 2, 0:1, :], lambda l: winds[l, 2, 0:1, :])
    receive_all(lon_copies)

    def first_row(i):
        odd = i % 2
        half = i // 2
        middle = pieces // 2
        return 2 * (odd * (middle + half) + (1 - odd) * (middle - 1 - half))

    mine = pl.ds(pl.multiple_of(g * own_tr, own_tr), own_tr)

    def forward_copy(i, k, part):
        r0 = first_row(i)
        part = pl.ds(pl.multiple_of(part * own_tr, own_tr), own_tr)
        return remote(
            adv.at[peers[k], pl.ds(r0, 2)],
            block.at[pl.ds(r0, 2), part],
            fwd_sem,
            (i, k),
            (peers[k], la, lo),
        )

    def advect(i, carry):
        r0 = first_row(i)
        for rr in range(2):
            r = r0 + rr
            for l in range(levels):
                q = l * rows + r

                def c(j):
                    return coef[j, l, pl.ds(r, 1), :]

                here = cells[l, r + 1]
                east_of = jnp.where(
                    lane == width - 1,
                    pltpu.roll(sides[1], width - 1 - q, 1),
                    pltpu.roll(here, width - 1, 1),
                )
                west_of = jnp.where(
                    lane == 0,
                    pltpu.roll(sides[0], lax.rem(width - q, width), 1),
                    pltpu.roll(here, 1, 1),
                )
                total = c(0) * here + c(1) * east_of + c(2) * west_of
                total = total + c(3) * cells[l, r + 2] + c(4) * cells[l, r]
                if l < levels - 1:
                    total = total + c(5) * cells[l + 1, r + 1]
                if l > 0:
                    total = total + c(6) * cells[l - 1, r + 1]
                adv[l, r] = total
            block[r, mine, :] = adv[g, r]
        for k in range(groups - 1):
            forward_copy(i, k, g).start()
        return carry

    lax.fori_loop(0, pieces - 2, advect, 0)

    await_answer(0)
    await_answer(1)
    start_lat(lat_copies, leads)
    start_lat(rim_copies, leads)
    for i in range(8, 13):
        loads[i].wait()
    t = own[3]
    misc[1] = 1.0 / (1.0 + jnp.exp(-2.0 * t))
    heat_b[...] = jnp.transpose(jnp.broadcast_to(heat_v[...], (species_all, species_all)))

    def back_copy(i, k, level):
        r0 = first_row(i)
        part = pl.ds(pl.multiple_of(peers[k] * own_tr, own_tr), own_tr)
        return remote(
            reacted.at[pl.ds(r0, 2), part],
            back.at[level, pl.ds(r0, 2)],
            back_sem,
            (i, k),
            (peers[k], la, lo),
        )

    twice = (la + 1) * rows > 3 * lats * rows // 4

    def react(i, carry):
        r0 = first_row(i)
        for k in range(groups - 1):
            forward_copy(i, k, lax.rem(g + groups - 1 - k, groups)).wait_recv()

        def pair_of(ref):
            return jnp.concatenate([ref[pl.ds(r0, 1), :], ref[pl.ds(r0 + 1, 1), :]], axis=1)

        rate = pair_of(misc.at[1])
        count = pair_of(count_v)

        def substep(current, counter):
            narrow = current.astype(jnp.bfloat16)
            pair_terms = jnp.dot(comp_v[...], narrow, preferred_element_type=jnp.float32)
            quad = (
                (pair_terms.reshape(repeats, species_all, 2 * width) * current[None])
                .reshape(repeats * species_all, 2 * width)
                .astype(jnp.bfloat16)
            )
            made = jnp.dot(stoi_v[...], quad, preferred_element_type=jnp.float32)
            later = current + chem_step * (rate * made - current)
            return jnp.where(counter < count, later, current)

        def load(ref):
            return jnp.concatenate([ref[r0], ref[r0 + 1]], axis=1)

        def keep(value):
            reacted[r0] = value[:, :width]
            reacted[r0 + 1] = value[:, width:]

        keep(substep(load(block), 0))

        @pl.when(twice)
        def _():
            keep(substep(load(reacted), 1))

        for k in range(groups - 1):
            back_copy(i, k, g).start()
        for rr in range(2):
            r = r0 + rr
            gain = heat_b[...] * (reacted[r] - block[r])
            misc[3, pl.ds(r, 1), :] = jnp.sum(gain, axis=0, keepdims=True)
        return carry

    lax.fori_loop(0, pieces // 2, react, 0)

    receive_all(rim_copies)
    receive_all(lat_copies)
    meridional(lambda l: rim_in[0, l : l + 1, :], lambda l: rim_in[1, l : l + 1, :])
    lax.fori_loop(pieces - 2, pieces, advect, 0)

    lax.fori_loop(pieces // 2, pieces, react, 0)

    receive_all(lonv_copies)

    def around(f, j, west_tile, east_tile):
        s, n = rim_in[0, levels + j : levels + j + 1, :], rim_in[1, levels + j : levels + j + 1, :]
        return from_east(f, east_tile), from_west(f, west_tile), from_north(f, n), from_south(f, s)

    t_e, t_w, t_n, t_s = around(t, 2, side_vt[0, 1], side_vt[1, 1])
    u = own[1]
    e, w, n, s = around(u, 0, side_u[0, g], side_u[1, g])
    east_out[0] = u + diffusion * (e + w + n + s - 4.0 * u) - pressure * (t_e - t_w)
    v = own[2]
    e, w, n, s = around(v, 1, side_vt[0, 0], side_vt[1, 0])
    north_out[0] = v + diffusion * (e + w + n + s - 4.0 * v) - pressure * (t_n - t_s)
    misc[2] = t + diffusion * (t_e + t_w + t_n + t_s - 4.0 * t)

    temp_out[0] = misc[2] + misc[3] / misc[0]

    def collect(i, carry):
        r0 = first_row(i)
        for k in range(groups - 1):
            back_copy(i, k, lax.rem(g + groups - 1 - k, groups)).wait_recv()
        for rr in range(2):
            back[g, r0 + rr] = reacted[r0 + rr, mine, :]
            for l in range(levels):
                at = l * rows + r0 + rr
                tracers[pl.ds(at, own_tr, stride=levels * rows), :] = back[l, r0 + rr]
        return carry

    lax.fori_loop(0, pieces, collect, 0)

    for sends, _, copy in lon_copies + lat_copies + lonv_copies + lonu_copies + rim_copies:
        pl.when(sends)(copy.wait_send)
    for k in range(groups - 1):
        wind_copy(k, g).wait_send()

    def finish(i, carry):
        for k in range(groups - 1):
            forward_copy(i, k, g).wait_send()
            back_copy(i, k, g).wait_send()
        return carry

    lax.fori_loop(0, pieces, finish, 0)


def store(tracers, east, north, temp, tracers_out, east_out, north_out, temp_out, sem):
    parts = sem.shape[0] - 3
    part = tracers.shape[0] // parts
    pairs = [(tracers.at[pl.ds(n * part, part)], tracers_out.at[pl.ds(n * part, part)]) for n in range(parts)]
    pairs += [(east, east_out), (north, north_out), (temp, temp_out)]
    copies = [pltpu.make_async_copy(src, dst, sem.at[i]) for i, (src, dst) in enumerate(pairs)]
    for copy in copies:
        copy.start()
    for copy in copies:
        copy.wait()


def local(sizes, species, east, north, up, warm, dens, counts, comp, stoi, heat):
    own_tr, levels, rows, width = species.shape
    all_tr, terms = stoi.shape
    groups = sizes[0]
    pieces = rows // 2
    f32 = jnp.float32
    dma = pltpu.SemaphoreType.DMA
    inputs = (
        species.reshape(own_tr * levels * rows, width),
        east,
        north,
        up,
        warm,
        dens,
        counts,
        comp,
        stoi,
        heat.reshape(1, all_tr),
    )
    tracers, east, north, temp = pl.pallas_call(
        functools.partial(kernel, sizes),
        out_shape=(pltpu.VMEM((own_tr * levels * rows, width), f32),)
        + (pltpu.VMEM((1, rows, width), f32),) * 3,
        in_specs=[pl.BlockSpec(memory_space=pltpu.HBM)] * 10,
        out_specs=[pl.BlockSpec(memory_space=pltpu.VMEM)] * 4,
        scratch_shapes=[
            pltpu.VMEM((own_tr * levels * rows, width), f32),
            pltpu.VMEM((levels, rows + 2, own_tr, width), f32),
            pltpu.VMEM((2, own_tr, width), f32),
            pltpu.VMEM((2, own_tr, width), f32),
            pltpu.VMEM((levels, rows, own_tr, width), f32),
            pltpu.VMEM((rows, all_tr, width), f32),
            pltpu.VMEM((rows, all_tr, width), f32),
            pltpu.VMEM((levels, rows, own_tr, width), f32),
            pltpu.VMEM((4, rows, width), f32),
            pltpu.VMEM((levels, 3, rows, width), f32),
            pltpu.VMEM((2, levels, rows, width), f32),
            pltpu.VMEM((2, 2, rows, width), f32),
            pltpu.VMEM((2, 8, width), f32),
            pltpu.VMEM((2, 8, width), f32),
            pltpu.VMEM((8, levels, rows, width), f32),
            pltpu.VMEM((4, rows, width), f32),
            pltpu.VMEM((rows, width), jnp.int32),
            pltpu.VMEM((terms, all_tr), jnp.bfloat16),
            pltpu.VMEM((all_tr, terms), jnp.bfloat16),
            pltpu.VMEM((1, all_tr), f32),
            pltpu.VMEM((all_tr, all_tr), f32),
            dma((13,)),
            dma((2, groups - 1)),
            dma((2, 2)),
            dma((2, 2)),
            dma((2, 2)),
            dma((2, 2)),
            dma((2, 2)),
            dma((2, pieces, groups - 1)),
            dma((2, pieces, groups - 1)),
            pltpu.SemaphoreType.REGULAR((4,)),
        ],
        compiler_params=pltpu.CompilerParams(
            collective_id=0, has_side_effects=True, vmem_limit_bytes=40 << 20
        ),
        name="couple",
    )(*(pltpu.with_memory_space_constraint(x, pltpu.HBM) for x in inputs))
    parts = 4
    results = (tracers, east, north, temp)
    tracers, east, north, temp = pl.pallas_call(
        store,
        out_shape=tuple(jax.ShapeDtypeStruct(x.shape, f32) for x in results),
        in_specs=[pl.BlockSpec(memory_space=pltpu.VMEM)] * 4,
        out_specs=[pl.BlockSpec(memory_space=pl.ANY)] * 4,
        scratch_shapes=[dma((parts + 3,))],
        compiler_params=pltpu.CompilerParams(vmem_limit_bytes=40 << 20),
        name="store",
    )(*(pltpu.with_memory_space_constraint(x, pltpu.VMEM) for x in results))
    return tracers.reshape(own_tr, levels, rows, width), east, north, temp


def solution(mesh):
    sizes = (mesh.shape["group"], mesh.shape["lat"], mesh.shape["lon"])
    fields = P("group", "lat", "lon")
    return jax.shard_map(
        functools.partial(local, sizes),
        mesh=mesh,
        in_specs=(
            P("group", None, "lat", "lon"),
            fields,
            fields,
            fields,
            fields,
            fields,
            P("lat", "lon"),
            P(),
            P(),
            P(),
        ),
        out_specs=(P("group", None, "lat", "lon"), fields, fields, fields),
        check_vma=False,
    )
```

```python
import functools

import jax
import jax.numpy as jnp
from jax import lax
from jax.experimental import pallas as pl
from jax.experimental.pallas import tpu as pltpu
from jax.sharding import PartitionSpec as P

MESH = pl.DeviceIdType.MESH
diffusion = 0.1
pressure = 0.05
chem_step = 0.2


def kernel(
    sizes,
    species,
    east,
    north,
    up,
    warm,
    dens,
    counts,
    comp,
    stoi,
    heat,
    tracers,
    east_out,
    north_out,
    temp_out,
    raw,
    cells,
    packs,
    edges,
    edges_in,
    fix,
    adv,
    block,
    reacted,
    back,
    own,
    winds,
    side_in,
    rim_out,
    rim_in,
    coef,
    misc,
    count_v,
    comp_v,
    stoi_v,
    heat_v,
    heat_b,
    load_sem,
    wind_sem,
    lat_sem,
    rim_sem,
    pack_sem,
    lon_sem,
    side_sem,
    fwd_sem,
    back_sem,
    ok_sem,
):
    groups, lats, lons = sizes
    g, la, lo = lax.axis_index("group"), lax.axis_index("lat"), lax.axis_index("lon")
    levels, rows, own_tr, width = adv.shape
    species_all = comp_v.shape[1]
    repeats = comp_v.shape[0] // species_all
    pieces = rows // 2
    peers = [lax.rem(g + k, groups) for k in range(1, groups)]
    has_s, has_n, has_w, has_e = la > 0, la < lats - 1, lo > 0, lo < lons - 1
    dev_s, dev_n, dev_w, dev_e = (g, la - 1, lo), (g, la + 1, lo), (g, la, lo - 1), (g, la, lo + 1)

    turned = la == 3 * lats // 4
    odd = lax.rem(lo, 2) == 1
    near = [
        (has_s, dev_s, turned),
        (has_n, dev_n, la != 3 * lats // 4 - 1),
        (has_w, dev_w, odd),
        (has_e, dev_e, odd),
    ]
    leads = [jnp.logical_and(has, lead) for has, _, lead in near]
    follows = [jnp.logical_and(has, jnp.logical_not(lead)) for has, _, lead in near]
    barrier = pltpu.get_barrier_semaphore()

    def greet(dev):
        pl.semaphore_signal(barrier, inc=1, device_id=dev, device_id_type=MESH)

    for p in peers:
        greet((p, la, lo))
    for lead, (_, dev, _) in zip(leads, near):
        pl.when(lead)(functools.partial(greet, dev))

    def answer(i):
        pl.semaphore_signal(
            ok_sem.at[i ^ 1], inc=1, device_id=near[i][1], device_id_type=MESH
        )

    def await_answer(i):
        pl.when(leads[i])(lambda: pl.semaphore_wait(ok_sem.at[i], 1))

    part = own_tr * levels * rows // 4
    loads = [
        pltpu.make_async_copy(src, dst, load_sem.at[i])
        for i, (src, dst) in enumerate(
            [
                (species.at[pl.ds(n * part, part)], raw.at[pl.ds(n * part, part)])
                for n in range(4)
            ]
            + [
                (up.at[0], own.at[0]),
                (east.at[0], own.at[1]),
                (north.at[0], own.at[2]),
                (warm.at[0], own.at[3]),
                (dens.at[0], misc.at[0]),
                (counts, count_v),
                (comp, comp_v),
                (stoi, stoi_v),
                (heat, heat_v),
            ]
        )
    ]
    for i in list(range(4, 8)) + list(range(4)) + list(range(8, 13)):
        loads[i].start()

    @pl.when(jnp.logical_not(has_s))
    def _():
        cells[:, 0] = jnp.zeros((levels, own_tr, width), jnp.float32)
        rim_in[0] = jnp.zeros((8, width), jnp.float32)

    @pl.when(jnp.logical_not(has_n))
    def _():
        cells[:, rows + 1] = jnp.zeros((levels, own_tr, width), jnp.float32)
        rim_in[1] = jnp.zeros((8, width), jnp.float32)

    @pl.when(jnp.logical_not(has_w))
    def _():
        edges_in[0] = jnp.zeros((species_all, width), jnp.float32)
        side_in[0] = jnp.zeros((3, rows, width), jnp.float32)

    @pl.when(jnp.logical_not(has_e))
    def _():
        edges_in[1] = jnp.zeros((species_all, width), jnp.float32)
        side_in[1] = jnp.zeros((3, rows, width), jnp.float32)

    pl.semaphore_wait(barrier, groups - 1 + sum(f.astype(jnp.int32) for f in follows))
    for i in range(4):
        pl.when(follows[i])(functools.partial(answer, i))

    def remote(src, dst, sems, index, dev):
        return pltpu.make_async_remote_copy(
            src_ref=src,
            dst_ref=dst,
            send_sem=sems.at[(0,) + index],
            recv_sem=sems.at[(1,) + index],
            device_id=dev,
            device_id_type=MESH,
        )

    def wind_copies(k, level):
        return [
            remote(field.at[0], winds.at[level, f], wind_sem, (f, k), (peers[k], la, lo))
            for f, field in enumerate((up, east, north))
        ]

    for k in range(groups - 1):
        for copy in wind_copies(k, g):
            copy.start()

    lane = lax.broadcasted_iota(jnp.int32, (own_tr, width), 1)

    for i in range(8):
        loads[i].wait()
    winds[g] = own[0:3]

    def turn(r, packed):
        done = []
        hit = jnp.logical_or(lane == 2 * r, lane == lax.rem(2 * r + width - 1, width))
        for l in range(levels):
            tile = raw[pl.ds(l * rows + r, own_tr, stride=levels * rows), :]
            cells[l, r + 1] = tile
            done.append(jnp.where(hit, pltpu.roll(tile, 2 * r, 1), packed[l]))
        return tuple(done)

    zero = jnp.zeros((own_tr, width), jnp.float32)
    for l, packed in enumerate(lax.fori_loop(0, rows, turn, (zero,) * levels)):
        packs[l] = packed

    mine = pl.ds(pl.multiple_of(g * own_tr, own_tr), own_tr)

    def part_of(group):
        return pl.ds(pl.multiple_of(group * own_tr, own_tr), own_tr)

    def pack_copy(k, group):
        return remote(
            packs.at[peers[k]], edges.at[part_of(group)], pack_sem, (k,), (peers[k], la, lo)
        )

    for k in range(groups - 1):
        pack_copy(k, g).start()
    edges[mine, :] = packs[g]
    lon_copies = [
        (has_e, has_w, remote(edges, edges_in.at[0], lon_sem, (0,), dev_e)),
        (has_w, has_e, remote(edges, edges_in.at[1], lon_sem, (1,), dev_w)),
    ]
    side_copies = [
        (has_e, has_w, remote(own.at[pl.ds(1, 3)], side_in.at[0], side_sem, (0,), dev_e)),
        (has_w, has_e, remote(own.at[pl.ds(1, 3)], side_in.at[1], side_sem, (1,), dev_w)),
    ]
    lat_copies = [
        (has_n, has_s, remote(cells.at[:, rows], cells.at[:, 0], lat_sem, (0,), dev_n)),
        (has_s, has_n, remote(cells.at[:, 1], cells.at[:, rows + 1], lat_sem, (1,), dev_s)),
    ]
    rim_copies = [
        (has_n, has_s, remote(rim_out.at[0], rim_in.at[0], rim_sem, (0,), dev_n)),
        (has_s, has_n, remote(rim_out.at[1], rim_in.at[1], rim_sem, (1,), dev_s)),
    ]

    def start_all(copies):
        for sends, _, copy in copies:
            pl.when(sends)(copy.start)

    def receive_all(copies):
        for _, receives, copy in copies:
            pl.when(receives)(copy.wait_recv)

    def start_lat(copies, which):
        pl.when(which[1])(copies[0][2].start)
        pl.when(which[0])(copies[1][2].start)

    start_lat(lat_copies, follows)

    for k in range(groups - 1):
        for copy in wind_copies(k, lax.rem(g + groups - 1 - k, groups)):
            copy.wait_recv()
    for l in range(levels):
        rim_out[0, l : l + 1, :] = winds[l, 2, rows - 1 : rows, :]
        rim_out[1, l : l + 1, :] = winds[l, 2, 0:1, :]
    for j in range(3):
        rim_out[0, levels + j : levels + j + 1, :] = own[1 + j, rows - 1 : rows, :]
        rim_out[1, levels + j : levels + j + 1, :] = own[1 + j, 0:1, :]
    start_lat(rim_copies, follows)

    row_at = lax.broadcasted_iota(jnp.int32, (rows, width), 0)
    lane_at = lax.broadcasted_iota(jnp.int32, (rows, width), 1)

    def from_west(f, edge):
        return jnp.where(lane_at == 0, pltpu.roll(edge, 1, 1), pltpu.roll(f, 1, 1))

    def from_east(f, edge):
        return jnp.where(
            lane_at == width - 1, pltpu.roll(edge, width - 1, 1), pltpu.roll(f, width - 1, 1)
        )

    def from_south(f, edge):
        return jnp.where(row_at == 0, edge, pltpu.roll(f, 1, 0))

    def from_north(f, edge):
        return jnp.where(row_at == rows - 1, edge, pltpu.roll(f, rows - 1, 0))

    def zonal_vertical():
        for l in range(levels):
            u = winds[l, 1]
            a_e = jnp.where(lane_at < width - 1, 0.5 * (u + pltpu.roll(u, width - 1, 1)), 0.0)
            a_w = jnp.where(lane_at > 0, 0.5 * (pltpu.roll(u, 1, 1) + u), 0.0)
            keep = 1.0 - jnp.maximum(a_e, 0.0) + jnp.minimum(a_w, 0.0)
            coef[1, l] = -jnp.minimum(a_e, 0.0)
            coef[2, l] = jnp.maximum(a_w, 0.0)
            if l < levels - 1:
                a_u = 0.5 * (winds[l, 0] + winds[l + 1, 0])
                keep = keep - jnp.maximum(a_u, 0.0)
                coef[5, l] = -jnp.minimum(a_u, 0.0)
            if l > 0:
                a_d = 0.5 * (winds[l - 1, 0] + winds[l, 0])
                keep = keep + jnp.minimum(a_d, 0.0)
                coef[6, l] = jnp.maximum(a_d, 0.0)
            coef[7, l] = keep

    def meridional(south_rim, north_rim):
        for l in range(levels):
            v = winds[l, 2]
            a_n = 0.5 * (v + from_north(v, north_rim(l)))
            a_s = 0.5 * (from_south(v, south_rim(l)) + v)
            coef[3, l] = -jnp.minimum(a_n, 0.0)
            coef[4, l] = jnp.maximum(a_s, 0.0)
            coef[0, l] = coef[7, l] - jnp.maximum(a_n, 0.0) + jnp.minimum(a_s, 0.0)

    zonal_vertical()
    meridional(lambda l: winds[l, 2, 0:1, :], lambda l: winds[l, 2, 0:1, :])
    def first_row(i):
        odd = i % 2
        half = i // 2
        middle = pieces // 2
        return 2 * (odd * (middle + half) + (1 - odd) * (middle - 1 - half))

    def forward_copy(i, k, part):
        r0 = first_row(i)
        part = part_of(part)
        return remote(
            adv.at[peers[k], pl.ds(r0, 2)],
            block.at[pl.ds(r0, 2), part],
            fwd_sem,
            (i, k),
            (peers[k], la, lo),
        )

    def advect(i, carry):
        r0 = first_row(i)
        for rr in range(2):
            r = r0 + rr
            for l in range(levels):

                def c(j):
                    return coef[j, l, pl.ds(r, 1), :]

                here = cells[l, r + 1]
                east_of = pltpu.roll(here, width - 1, 1)
                west_of = pltpu.roll(here, 1, 1)
                total = c(0) * here + c(1) * east_of + c(2) * west_of
                total = total + c(3) * cells[l, r + 2] + c(4) * cells[l, r]
                if l < levels - 1:
                    total = total + c(5) * cells[l + 1, r + 1]
                if l > 0:
                    total = total + c(6) * cells[l - 1, r + 1]
                adv[l, r] = total
            block[r, mine, :] = adv[g, r]
        for k in range(groups - 1):
            forward_copy(i, k, g).start()
        return carry

    lax.fori_loop(0, 2, advect, 0)

    for k in range(groups - 1):
        pack_copy(k, lax.rem(g + groups - 1 - k, groups)).wait_recv()
    await_answer(3)
    pl.when(has_e)(side_copies[0][2].start)
    pl.when(has_e)(lon_copies[0][2].start)
    await_answer(2)
    pl.when(has_w)(side_copies[1][2].start)
    pl.when(has_w)(lon_copies[1][2].start)

    lax.fori_loop(2, pieces - 2, advect, 0)

    await_answer(0)
    await_answer(1)
    start_lat(lat_copies, leads)
    start_lat(rim_copies, leads)
    for i in range(8, 13):
        loads[i].wait()
    t = own[3]
    misc[1] = 1.0 / (1.0 + jnp.exp(-2.0 * t))
    heat_b[...] = jnp.transpose(jnp.broadcast_to(heat_v[...], (species_all, species_all)))

    def back_copy(i, k, level):
        r0 = first_row(i)
        part = part_of(peers[k])
        return remote(
            reacted.at[pl.ds(r0, 2), part],
            back.at[level, pl.ds(r0, 2)],
            back_sem,
            (i, k),
            (peers[k], la, lo),
        )

    receive_all(side_copies)
    u = own[1]
    a_w = 0.5 * (from_west(u, side_in[0, 0]) + u)
    a_e = 0.5 * (u + from_east(u, side_in[1, 0]))
    a_w = jnp.where(lane_at == 2 * row_at, a_w[:, 0:1], 0.0)
    a_e = jnp.where(lane_at == lax.rem(2 * row_at + width - 1, width), a_e[:, width - 1 :], 0.0)
    a = jnp.sum(a_w + a_e, axis=0, keepdims=True)
    receive_all(lon_copies)
    first_lane = lax.rem(lax.broadcasted_iota(jnp.int32, (species_all, width), 1), 2) == 0
    beyond = jnp.where(
        first_lane, pltpu.roll(edges_in[0], 1, 1), pltpu.roll(edges_in[1], width - 1, 1)
    )
    here = edges[...]
    more, less = jnp.maximum(a, 0.0), jnp.minimum(a, 0.0)
    fix[...] = jnp.where(first_lane, more * beyond + less * here, -(more * here + less * beyond))

    twice = (la + 1) * rows > 3 * lats * rows // 4

    def react(i, carry):
        r0 = first_row(i)
        for k in range(groups - 1):
            forward_copy(i, k, lax.rem(g + groups - 1 - k, groups)).wait_recv()

        def pair_of(ref):
            return jnp.concatenate([ref[pl.ds(r0, 1), :], ref[pl.ds(r0 + 1, 1), :]], axis=1)

        rate = pair_of(misc.at[1])
        count = pair_of(count_v)

        def substep(current, counter):
            narrow = current.astype(jnp.bfloat16)
            pair_terms = jnp.dot(comp_v[...], narrow, preferred_element_type=jnp.float32)
            quad = (
                (pair_terms.reshape(repeats, species_all, 2 * width) * current[None])
                .reshape(repeats * species_all, 2 * width)
                .astype(jnp.bfloat16)
            )
            made = jnp.dot(stoi_v[...], quad, preferred_element_type=jnp.float32)
            later = current + chem_step * (rate * made - current)
            return jnp.where(counter < count, later, current)

        def load(ref):
            return jnp.concatenate([ref[r0], ref[r0 + 1]], axis=1)

        at_edge = lax.broadcasted_iota(jnp.int32, (species_all, width), 1)
        at_edge = jnp.logical_or(at_edge == 0, at_edge == width - 1)
        for r in (r0, r0 + 1):
            moved = pltpu.roll(fix[...], lax.rem(width - 2 * r, width), 1)
            block[r] = block[r] + jnp.where(at_edge, moved, 0.0)

        def keep(value):
            reacted[r0] = value[:, :width]
            reacted[r0 + 1] = value[:, width:]

        keep(substep(load(block), 0))

        @pl.when(twice)
        def _():
            keep(substep(load(reacted), 1))

        for k in range(groups - 1):
            back_copy(i, k, g).start()
        for rr in range(2):
            r = r0 + rr
            gain = heat_b[...] * (reacted[r] - block[r])
            misc[3, pl.ds(r, 1), :] = jnp.sum(gain, axis=0, keepdims=True)
        return carry

    lax.fori_loop(0, 3, react, 0)

    receive_all(rim_copies)
    receive_all(lat_copies)
    meridional(lambda l: rim_in[0, l : l + 1, :], lambda l: rim_in[1, l : l + 1, :])
    lax.fori_loop(pieces - 2, pieces, advect, 0)

    lax.fori_loop(3, pieces, react, 0)


    def around(f, j, west_tile, east_tile):
        s, n = rim_in[0, levels + j : levels + j + 1, :], rim_in[1, levels + j : levels + j + 1, :]
        return from_east(f, east_tile), from_west(f, west_tile), from_north(f, n), from_south(f, s)

    t_e, t_w, t_n, t_s = around(t, 2, side_in[0, 2], side_in[1, 2])
    u = own[1]
    e, w, n, s = around(u, 0, side_in[0, 0], side_in[1, 0])
    east_out[0] = u + diffusion * (e + w + n + s - 4.0 * u) - pressure * (t_e - t_w)
    v = own[2]
    e, w, n, s = around(v, 1, side_in[0, 1], side_in[1, 1])
    north_out[0] = v + diffusion * (e + w + n + s - 4.0 * v) - pressure * (t_n - t_s)
    misc[2] = t + diffusion * (t_e + t_w + t_n + t_s - 4.0 * t)

    temp_out[0] = misc[2] + misc[3] / misc[0]

    def collect(i, carry):
        r0 = first_row(i)
        for k in range(groups - 1):
            back_copy(i, k, lax.rem(g + groups - 1 - k, groups)).wait_recv()
        for rr in range(2):
            back[g, r0 + rr] = reacted[r0 + rr, mine, :]
            for l in range(levels):
                at = l * rows + r0 + rr
                tracers[pl.ds(at, own_tr, stride=levels * rows), :] = back[l, r0 + rr]
        return carry

    lax.fori_loop(0, pieces, collect, 0)

    for sends, _, copy in lon_copies + lat_copies + side_copies + rim_copies:
        pl.when(sends)(copy.wait_send)
    for k in range(groups - 1):
        for copy in wind_copies(k, g):
            copy.wait_send()
        pack_copy(k, g).wait_send()

    def finish(i, carry):
        for k in range(groups - 1):
            forward_copy(i, k, g).wait_send()
            back_copy(i, k, g).wait_send()
        return carry

    lax.fori_loop(0, pieces, finish, 0)


def store(tracers, east, north, temp, tracers_out, east_out, north_out, temp_out, sem):
    parts = sem.shape[0] - 3
    part = tracers.shape[0] // parts
    pairs = [(tracers.at[pl.ds(n * part, part)], tracers_out.at[pl.ds(n * part, part)]) for n in range(parts)]
    pairs += [(east, east_out), (north, north_out), (temp, temp_out)]
    copies = [pltpu.make_async_copy(src, dst, sem.at[i]) for i, (src, dst) in enumerate(pairs)]
    for copy in copies:
        copy.start()
    for copy in copies:
        copy.wait()


def local(sizes, species, east, north, up, warm, dens, counts, comp, stoi, heat):
    own_tr, levels, rows, width = species.shape
    all_tr, terms = stoi.shape
    groups = sizes[0]
    pieces = rows // 2
    f32 = jnp.float32
    dma = pltpu.SemaphoreType.DMA
    inputs = (
        species.reshape(own_tr * levels * rows, width),
        east,
        north,
        up,
        warm,
        dens,
        counts,
        comp,
        stoi,
        heat.reshape(1, all_tr),
    )
    tracers, east, north, temp = pl.pallas_call(
        functools.partial(kernel, sizes),
        out_shape=(pltpu.VMEM((own_tr * levels * rows, width), f32),)
        + (pltpu.VMEM((1, rows, width), f32),) * 3,
        in_specs=[pl.BlockSpec(memory_space=pltpu.HBM)] * 10,
        out_specs=[pl.BlockSpec(memory_space=pltpu.VMEM)] * 4,
        scratch_shapes=[
            pltpu.VMEM((own_tr * levels * rows, width), f32),
            pltpu.VMEM((levels, rows + 2, own_tr, width), f32),
            pltpu.VMEM((levels, own_tr, width), f32),
            pltpu.VMEM((all_tr, width), f32),
            pltpu.VMEM((2, all_tr, width), f32),
            pltpu.VMEM((all_tr, width), f32),
            pltpu.VMEM((levels, rows, own_tr, width), f32),
            pltpu.VMEM((rows, all_tr, width), f32),
            pltpu.VMEM((rows, all_tr, width), f32),
            pltpu.VMEM((levels, rows, own_tr, width), f32),
            pltpu.VMEM((4, rows, width), f32),
            pltpu.VMEM((levels, 3, rows, width), f32),
            pltpu.VMEM((2, 3, rows, width), f32),
            pltpu.VMEM((2, 8, width), f32),
            pltpu.VMEM((2, 8, width), f32),
            pltpu.VMEM((8, levels, rows, width), f32),
            pltpu.VMEM((4, rows, width), f32),
            pltpu.VMEM((rows, width), jnp.int32),
            pltpu.VMEM((terms, all_tr), jnp.bfloat16),
            pltpu.VMEM((all_tr, terms), jnp.bfloat16),
            pltpu.VMEM((1, all_tr), f32),
            pltpu.VMEM((all_tr, all_tr), f32),
            dma((13,)),
            dma((2, 3, groups - 1)),
            dma((2, 2)),
            dma((2, 2)),
            dma((2, groups - 1)),
            dma((2, 2)),
            dma((2, 2)),
            dma((2, pieces, groups - 1)),
            dma((2, pieces, groups - 1)),
            pltpu.SemaphoreType.REGULAR((4,)),
        ],
        compiler_params=pltpu.CompilerParams(
            collective_id=0, has_side_effects=True, vmem_limit_bytes=40 << 20
        ),
        name="couple",
    )(*(pltpu.with_memory_space_constraint(x, pltpu.HBM) for x in inputs))
    parts = 4
    results = (tracers, east, north, temp)
    tracers, east, north, temp = pl.pallas_call(
        store,
        out_shape=tuple(jax.ShapeDtypeStruct(x.shape, f32) for x in results),
        in_specs=[pl.BlockSpec(memory_space=pltpu.VMEM)] * 4,
        out_specs=[pl.BlockSpec(memory_space=pl.ANY)] * 4,
        scratch_shapes=[dma((parts + 3,))],
        compiler_params=pltpu.CompilerParams(vmem_limit_bytes=40 << 20),
        name="store",
    )(*(pltpu.with_memory_space_constraint(x, pltpu.VMEM) for x in results))
    return tracers.reshape(own_tr, levels, rows, width), east, north, temp


def solution(mesh):
    sizes = (mesh.shape["group"], mesh.shape["lat"], mesh.shape["lon"])
    fields = P("group", "lat", "lon")
    return jax.shard_map(
        functools.partial(local, sizes),
        mesh=mesh,
        in_specs=(
            P("group", None, "lat", "lon"),
            fields,
            fields,
            fields,
            fields,
            fields,
            P("lat", "lon"),
            P(),
            P(),
            P(),
        ),
        out_specs=(P("group", None, "lat", "lon"), fields, fields, fields),
        check_vma=False,
    )
```

```python
import functools

import jax
import jax.numpy as jnp
from jax import lax
from jax.experimental import pallas as pl
from jax.experimental.pallas import tpu as pltpu
from jax.sharding import PartitionSpec as P

MESH = pl.DeviceIdType.MESH
diffusion = 0.1
pressure = 0.05
chem_step = 0.2


def kernel(
    sizes,
    species,
    east,
    north,
    up,
    warm,
    dens,
    counts,
    comp,
    stoi,
    heat,
    tracers,
    east_out,
    north_out,
    temp_out,
    raw,
    cells,
    packs,
    edges,
    edges_in,
    fix,
    adv,
    block,
    reacted,
    back,
    own,
    winds,
    side_in,
    rim_out,
    rim_in,
    coef,
    misc,
    count_v,
    comp_v,
    stoi_v,
    heat_v,
    heat_b,
    load_sem,
    wind_sem,
    lat_sem,
    rim_sem,
    pack_sem,
    lon_sem,
    side_sem,
    fwd_sem,
    back_sem,
    ok_sem,
):
    groups, lats, lons = sizes
    g, la, lo = lax.axis_index("group"), lax.axis_index("lat"), lax.axis_index("lon")
    levels, rows, own_tr, width = adv.shape
    species_all = comp_v.shape[1]
    repeats = comp_v.shape[0] // species_all
    pieces = rows // 2
    peers = [lax.rem(g + k, groups) for k in range(1, groups)]
    far_first = sorted(range(groups - 1), key=lambda k: -min(k + 1, groups - 1 - k))
    has_s, has_n, has_w, has_e = la > 0, la < lats - 1, lo > 0, lo < lons - 1
    dev_s, dev_n, dev_w, dev_e = (g, la - 1, lo), (g, la + 1, lo), (g, la, lo - 1), (g, la, lo + 1)

    turned = la == 3 * lats // 4
    odd = lax.rem(lo, 2) == 1
    near = [
        (has_s, dev_s, turned),
        (has_n, dev_n, la != 3 * lats // 4 - 1),
        (has_w, dev_w, odd),
        (has_e, dev_e, odd),
    ]
    leads = [jnp.logical_and(has, lead) for has, _, lead in near]
    follows = [jnp.logical_and(has, jnp.logical_not(lead)) for has, _, lead in near]
    barrier = pltpu.get_barrier_semaphore()

    def greet(dev):
        pl.semaphore_signal(barrier, inc=1, device_id=dev, device_id_type=MESH)

    for p in peers:
        greet((p, la, lo))
    for lead, (_, dev, _) in zip(leads, near):
        pl.when(lead)(functools.partial(greet, dev))

    def answer(i):
        pl.semaphore_signal(
            ok_sem.at[i ^ 1], inc=1, device_id=near[i][1], device_id_type=MESH
        )

    def await_answer(i):
        pl.when(leads[i])(lambda: pl.semaphore_wait(ok_sem.at[i], 1))

    part = own_tr * levels * rows // 4
    loads = [
        pltpu.make_async_copy(src, dst, load_sem.at[i])
        for i, (src, dst) in enumerate(
            [
                (species.at[pl.ds(n * part, part)], raw.at[pl.ds(n * part, part)])
                for n in range(4)
            ]
            + [
                (up.at[0], own.at[0]),
                (east.at[0], own.at[1]),
                (north.at[0], own.at[2]),
                (warm.at[0], own.at[3]),
                (dens.at[0], misc.at[0]),
                (counts, count_v),
                (comp, comp_v),
                (stoi, stoi_v),
                (heat, heat_v),
            ]
        )
    ]
    for i in list(range(4, 8)) + list(range(4)) + list(range(8, 13)):
        loads[i].start()

    @pl.when(jnp.logical_not(has_s))
    def _():
        cells[:, 0] = jnp.zeros((levels, own_tr, width), jnp.float32)
        rim_in[0] = jnp.zeros((8, width), jnp.float32)

    @pl.when(jnp.logical_not(has_n))
    def _():
        cells[:, rows + 1] = jnp.zeros((levels, own_tr, width), jnp.float32)
        rim_in[1] = jnp.zeros((8, width), jnp.float32)

    @pl.when(jnp.logical_not(has_w))
    def _():
        edges_in[0] = jnp.zeros((species_all, width), jnp.float32)
        side_in[0] = jnp.zeros((3, rows, width), jnp.float32)

    @pl.when(jnp.logical_not(has_e))
    def _():
        edges_in[1] = jnp.zeros((species_all, width), jnp.float32)
        side_in[1] = jnp.zeros((3, rows, width), jnp.float32)

    for i in range(4, 7):
        loads[i].wait()
    pl.semaphore_wait(barrier, groups - 1 + sum(f.astype(jnp.int32) for f in follows))
    for i in range(4):
        pl.when(follows[i])(functools.partial(answer, i))

    def remote(src, dst, sems, index, dev):
        return pltpu.make_async_remote_copy(
            src_ref=src,
            dst_ref=dst,
            send_sem=sems.at[(0,) + index],
            recv_sem=sems.at[(1,) + index],
            device_id=dev,
            device_id_type=MESH,
        )

    def wind_copies(k, level):
        return [
            remote(own.at[f], winds.at[level, f], wind_sem, (f, k), (peers[k], la, lo))
            for f in range(3)
        ]

    for k in far_first:
        for copy in wind_copies(k, g):
            copy.start()

    lane = lax.broadcasted_iota(jnp.int32, (own_tr, width), 1)

    for i in (0, 1, 2, 3, 7):
        loads[i].wait()
    winds[g] = own[0:3]

    def turn(r, packed):
        done = []
        hit = jnp.logical_or(lane == 2 * r, lane == lax.rem(2 * r + width - 1, width))
        for l in range(levels):
            tile = raw[pl.ds(l * rows + r, own_tr, stride=levels * rows), :]
            cells[l, r + 1] = tile
            done.append(jnp.where(hit, pltpu.roll(tile, 2 * r, 1), packed[l]))
        return tuple(done)

    zero = jnp.zeros((own_tr, width), jnp.float32)
    for l, packed in enumerate(lax.fori_loop(0, rows, turn, (zero,) * levels)):
        packs[l] = packed

    mine = pl.ds(pl.multiple_of(g * own_tr, own_tr), own_tr)

    def part_of(group):
        return pl.ds(pl.multiple_of(group * own_tr, own_tr), own_tr)

    def pack_copy(k, group):
        return remote(
            packs.at[peers[k]], edges.at[part_of(group)], pack_sem, (k,), (peers[k], la, lo)
        )

    for k in far_first:
        pack_copy(k, g).start()
    edges[mine, :] = packs[g]
    lon_copies = [
        (has_e, has_w, remote(edges, edges_in.at[0], lon_sem, (0,), dev_e)),
        (has_w, has_e, remote(edges, edges_in.at[1], lon_sem, (1,), dev_w)),
    ]
    side_copies = [
        (has_e, has_w, remote(own.at[pl.ds(1, 3)], side_in.at[0], side_sem, (0,), dev_e)),
        (has_w, has_e, remote(own.at[pl.ds(1, 3)], side_in.at[1], side_sem, (1,), dev_w)),
    ]
    lat_copies = [
        (has_n, has_s, remote(cells.at[:, rows], cells.at[:, 0], lat_sem, (0,), dev_n)),
        (has_s, has_n, remote(cells.at[:, 1], cells.at[:, rows + 1], lat_sem, (1,), dev_s)),
    ]
    rim_copies = [
        (has_n, has_s, remote(rim_out.at[0], rim_in.at[0], rim_sem, (0,), dev_n)),
        (has_s, has_n, remote(rim_out.at[1], rim_in.at[1], rim_sem, (1,), dev_s)),
    ]

    def start_all(copies):
        for sends, _, copy in copies:
            pl.when(sends)(copy.start)

    def receive_all(copies):
        for _, receives, copy in copies:
            pl.when(receives)(copy.wait_recv)

    def start_lat(copies, which):
        pl.when(which[1])(copies[0][2].start)
        pl.when(which[0])(copies[1][2].start)

    start_lat(lat_copies, follows)

    for k in range(groups - 1):
        for copy in wind_copies(k, lax.rem(g + groups - 1 - k, groups)):
            copy.wait_recv()
    for l in range(levels):
        rim_out[0, l : l + 1, :] = winds[l, 2, rows - 1 : rows, :]
        rim_out[1, l : l + 1, :] = winds[l, 2, 0:1, :]
    for j in range(3):
        rim_out[0, levels + j : levels + j + 1, :] = own[1 + j, rows - 1 : rows, :]
        rim_out[1, levels + j : levels + j + 1, :] = own[1 + j, 0:1, :]
    start_lat(rim_copies, follows)

    row_at = lax.broadcasted_iota(jnp.int32, (rows, width), 0)
    lane_at = lax.broadcasted_iota(jnp.int32, (rows, width), 1)

    def from_west(f, edge):
        return jnp.where(lane_at == 0, pltpu.roll(edge, 1, 1), pltpu.roll(f, 1, 1))

    def from_east(f, edge):
        return jnp.where(
            lane_at == width - 1, pltpu.roll(edge, width - 1, 1), pltpu.roll(f, width - 1, 1)
        )

    def from_south(f, edge):
        return jnp.where(row_at == 0, edge, pltpu.roll(f, 1, 0))

    def from_north(f, edge):
        return jnp.where(row_at == rows - 1, edge, pltpu.roll(f, rows - 1, 0))

    def zonal_vertical():
        for l in range(levels):
            u = winds[l, 1]
            a_e = jnp.where(lane_at < width - 1, 0.5 * (u + pltpu.roll(u, width - 1, 1)), 0.0)
            a_w = jnp.where(lane_at > 0, 0.5 * (pltpu.roll(u, 1, 1) + u), 0.0)
            keep = 1.0 - jnp.maximum(a_e, 0.0) + jnp.minimum(a_w, 0.0)
            coef[1, l] = -jnp.minimum(a_e, 0.0)
            coef[2, l] = jnp.maximum(a_w, 0.0)
            if l < levels - 1:
                a_u = 0.5 * (winds[l, 0] + winds[l + 1, 0])
                keep = keep - jnp.maximum(a_u, 0.0)
                coef[5, l] = -jnp.minimum(a_u, 0.0)
            if l > 0:
                a_d = 0.5 * (winds[l - 1, 0] + winds[l, 0])
                keep = keep + jnp.minimum(a_d, 0.0)
                coef[6, l] = jnp.maximum(a_d, 0.0)
            coef[7, l] = keep

    def meridional(south_rim, north_rim):
        for l in range(levels):
            v = winds[l, 2]
            a_n = 0.5 * (v + from_north(v, north_rim(l)))
            a_s = 0.5 * (from_south(v, south_rim(l)) + v)
            coef[3, l] = -jnp.minimum(a_n, 0.0)
            coef[4, l] = jnp.maximum(a_s, 0.0)
            coef[0, l] = coef[7, l] - jnp.maximum(a_n, 0.0) + jnp.minimum(a_s, 0.0)

    zonal_vertical()
    meridional(lambda l: winds[l, 2, 0:1, :], lambda l: winds[l, 2, 0:1, :])
    def first_row(i):
        odd = i % 2
        half = i // 2
        middle = pieces // 2
        return 2 * (odd * (middle + half) + (1 - odd) * (middle - 1 - half))

    def forward_copy(i, k, part):
        r0 = first_row(i)
        part = part_of(part)
        return remote(
            adv.at[peers[k], pl.ds(r0, 2)],
            block.at[pl.ds(r0, 2), part],
            fwd_sem,
            (i, k),
            (peers[k], la, lo),
        )

    def advect(i, carry):
        r0 = first_row(i)
        for rr in range(2):
            r = r0 + rr
            for l in range(levels):

                def c(j):
                    return coef[j, l, pl.ds(r, 1), :]

                here = cells[l, r + 1]
                east_of = pltpu.roll(here, width - 1, 1)
                west_of = pltpu.roll(here, 1, 1)
                total = c(0) * here + c(1) * east_of + c(2) * west_of
                total = total + c(3) * cells[l, r + 2] + c(4) * cells[l, r]
                if l < levels - 1:
                    total = total + c(5) * cells[l + 1, r + 1]
                if l > 0:
                    total = total + c(6) * cells[l - 1, r + 1]
                adv[l, r] = total
            block[r, mine, :] = adv[g, r]
        for k in far_first:
            forward_copy(i, k, g).start()
        return carry

    lax.fori_loop(0, 2, advect, 0)

    for k in range(groups - 1):
        pack_copy(k, lax.rem(g + groups - 1 - k, groups)).wait_recv()
    await_answer(3)
    pl.when(has_e)(side_copies[0][2].start)
    pl.when(has_e)(lon_copies[0][2].start)
    await_answer(2)
    pl.when(has_w)(side_copies[1][2].start)
    pl.when(has_w)(lon_copies[1][2].start)

    lax.fori_loop(2, pieces - 2, advect, 0)

    await_answer(0)
    await_answer(1)
    start_lat(lat_copies, leads)
    start_lat(rim_copies, leads)
    for i in range(8, 13):
        loads[i].wait()
    t = own[3]
    misc[1] = 1.0 / (1.0 + jnp.exp(-2.0 * t))
    heat_b[...] = jnp.transpose(jnp.broadcast_to(heat_v[...], (species_all, species_all)))

    def back_copy(i, k, level):
        r0 = first_row(i)
        part = part_of(peers[k])
        return remote(
            reacted.at[pl.ds(r0, 2), part],
            back.at[level, pl.ds(r0, 2)],
            back_sem,
            (i, k),
            (peers[k], la, lo),
        )

    receive_all(side_copies)
    u = own[1]
    a_w = 0.5 * (from_west(u, side_in[0, 0]) + u)
    a_e = 0.5 * (u + from_east(u, side_in[1, 0]))
    a_w = jnp.where(lane_at == 2 * row_at, a_w[:, 0:1], 0.0)
    a_e = jnp.where(lane_at == lax.rem(2 * row_at + width - 1, width), a_e[:, width - 1 :], 0.0)
    a = jnp.sum(a_w + a_e, axis=0, keepdims=True)
    receive_all(lon_copies)
    first_lane = lax.rem(lax.broadcasted_iota(jnp.int32, (species_all, width), 1), 2) == 0
    beyond = jnp.where(
        first_lane, pltpu.roll(edges_in[0], 1, 1), pltpu.roll(edges_in[1], width - 1, 1)
    )
    here = edges[...]
    more, less = jnp.maximum(a, 0.0), jnp.minimum(a, 0.0)
    fix[...] = jnp.where(first_lane, more * beyond + less * here, -(more * here + less * beyond))

    twice = (la + 1) * rows > 3 * lats * rows // 4

    def react(i, carry):
        r0 = first_row(i)
        for k in range(groups - 1):
            forward_copy(i, k, lax.rem(g + groups - 1 - k, groups)).wait_recv()

        def pair_of(ref):
            return jnp.concatenate([ref[pl.ds(r0, 1), :], ref[pl.ds(r0 + 1, 1), :]], axis=1)

        rate = pair_of(misc.at[1])
        count = pair_of(count_v)

        def substep(current, counter):
            narrow = current.astype(jnp.bfloat16)
            pair_terms = jnp.dot(comp_v[...], narrow, preferred_element_type=jnp.float32)
            quad = (
                (pair_terms.reshape(repeats, species_all, 2 * width) * current[None])
                .reshape(repeats * species_all, 2 * width)
                .astype(jnp.bfloat16)
            )
            made = jnp.dot(stoi_v[...], quad, preferred_element_type=jnp.float32)
            later = current + chem_step * (rate * made - current)
            return jnp.where(counter < count, later, current)

        def load(ref):
            return jnp.concatenate([ref[r0], ref[r0 + 1]], axis=1)

        at_edge = lax.broadcasted_iota(jnp.int32, (species_all, width), 1)
        at_edge = jnp.logical_or(at_edge == 0, at_edge == width - 1)
        for r in (r0, r0 + 1):
            moved = pltpu.roll(fix[...], lax.rem(width - 2 * r, width), 1)
            block[r] = block[r] + jnp.where(at_edge, moved, 0.0)

        def keep(value):
            reacted[r0] = value[:, :width]
            reacted[r0 + 1] = value[:, width:]

        keep(substep(load(block), 0))

        @pl.when(twice)
        def _():
            keep(substep(load(reacted), 1))

        for k in far_first:
            back_copy(i, k, g).start()
        for rr in range(2):
            r = r0 + rr
            gain = heat_b[...] * (reacted[r] - block[r])
            misc[3, pl.ds(r, 1), :] = jnp.sum(gain, axis=0, keepdims=True)
        return carry

    far = jnp.logical_or(jnp.logical_and(lax.rem(la, 4) == 3, has_n), jnp.logical_and(lax.rem(la, 4) == 0, has_s))
    early = jnp.where(far, 3, 0)
    lax.fori_loop(0, early, react, 0)

    receive_all(rim_copies)
    receive_all(lat_copies)
    meridional(lambda l: rim_in[0, l : l + 1, :], lambda l: rim_in[1, l : l + 1, :])
    lax.fori_loop(pieces - 2, pieces, advect, 0)

    lax.fori_loop(early, pieces, react, 0)


    def around(f, j, west_tile, east_tile):
        s, n = rim_in[0, levels + j : levels + j + 1, :], rim_in[1, levels + j : levels + j + 1, :]
        return from_east(f, east_tile), from_west(f, west_tile), from_north(f, n), from_south(f, s)

    t_e, t_w, t_n, t_s = around(t, 2, side_in[0, 2], side_in[1, 2])
    u = own[1]
    e, w, n, s = around(u, 0, side_in[0, 0], side_in[1, 0])
    east_out[0] = u + diffusion * (e + w + n + s - 4.0 * u) - pressure * (t_e - t_w)
    v = own[2]
    e, w, n, s = around(v, 1, side_in[0, 1], side_in[1, 1])
    north_out[0] = v + diffusion * (e + w + n + s - 4.0 * v) - pressure * (t_n - t_s)
    misc[2] = t + diffusion * (t_e + t_w + t_n + t_s - 4.0 * t)

    temp_out[0] = misc[2] + misc[3] / misc[0]

    for sends, _, copy in lon_copies + lat_copies + side_copies + rim_copies:
        pl.when(sends)(copy.wait_send)
    for k in range(groups - 1):
        for copy in wind_copies(k, g):
            copy.wait_send()
        pack_copy(k, g).wait_send()

    def collect(i, carry):
        r0 = first_row(i)
        for k in range(groups - 1):
            forward_copy(i, k, g).wait_send()
            back_copy(i, k, g).wait_send()
        for rr in range(2):
            back[g, r0 + rr] = reacted[r0 + rr, mine, :]
        for k in range(groups - 1):
            back_copy(i, k, lax.rem(g + groups - 1 - k, groups)).wait_recv()
        for rr in range(2):
            for l in range(levels):
                at = l * rows + r0 + rr
                tracers[pl.ds(at, own_tr, stride=levels * rows), :] = back[l, r0 + rr]
        return carry

    lax.fori_loop(0, pieces, collect, 0)


def store(tracers, east, north, temp, tracers_out, east_out, north_out, temp_out, sem):
    parts = sem.shape[0] - 3
    part = tracers.shape[0] // parts
    pairs = [(tracers.at[pl.ds(n * part, part)], tracers_out.at[pl.ds(n * part, part)]) for n in range(parts)]
    pairs += [(east, east_out), (north, north_out), (temp, temp_out)]
    copies = [pltpu.make_async_copy(src, dst, sem.at[i]) for i, (src, dst) in enumerate(pairs)]
    for copy in copies:
        copy.start()
    for copy in copies:
        copy.wait()


def local(sizes, species, east, north, up, warm, dens, counts, comp, stoi, heat):
    own_tr, levels, rows, width = species.shape
    all_tr, terms = stoi.shape
    groups = sizes[0]
    pieces = rows // 2
    f32 = jnp.float32
    dma = pltpu.SemaphoreType.DMA
    inputs = (
        species.reshape(own_tr * levels * rows, width),
        east,
        north,
        up,
        warm,
        dens,
        counts,
        comp,
        stoi,
        heat.reshape(1, all_tr),
    )
    tracers, east, north, temp = pl.pallas_call(
        functools.partial(kernel, sizes),
        out_shape=(pltpu.VMEM((own_tr * levels * rows, width), f32),)
        + (pltpu.VMEM((1, rows, width), f32),) * 3,
        in_specs=[pl.BlockSpec(memory_space=pltpu.HBM)] * 10,
        out_specs=[pl.BlockSpec(memory_space=pltpu.VMEM)] * 4,
        scratch_shapes=[
            pltpu.VMEM((own_tr * levels * rows, width), f32),
            pltpu.VMEM((levels, rows + 2, own_tr, width), f32),
            pltpu.VMEM((levels, own_tr, width), f32),
            pltpu.VMEM((all_tr, width), f32),
            pltpu.VMEM((2, all_tr, width), f32),
            pltpu.VMEM((all_tr, width), f32),
            pltpu.VMEM((levels, rows, own_tr, width), f32),
            pltpu.VMEM((rows, all_tr, width), f32),
            pltpu.VMEM((rows, all_tr, width), f32),
            pltpu.VMEM((levels, rows, own_tr, width), f32),
            pltpu.VMEM((4, rows, width), f32),
            pltpu.VMEM((levels, 3, rows, width), f32),
            pltpu.VMEM((2, 3, rows, width), f32),
            pltpu.VMEM((2, 8, width), f32),
            pltpu.VMEM((2, 8, width), f32),
            pltpu.VMEM((8, levels, rows, width), f32),
            pltpu.VMEM((4, rows, width), f32),
            pltpu.VMEM((rows, width), jnp.int32),
            pltpu.VMEM((terms, all_tr), jnp.bfloat16),
            pltpu.VMEM((all_tr, terms), jnp.bfloat16),
            pltpu.VMEM((1, all_tr), f32),
            pltpu.VMEM((all_tr, all_tr), f32),
            dma((13,)),
            dma((2, 3, groups - 1)),
            dma((2, 2)),
            dma((2, 2)),
            dma((2, groups - 1)),
            dma((2, 2)),
            dma((2, 2)),
            dma((2, pieces, groups - 1)),
            dma((2, pieces, groups - 1)),
            pltpu.SemaphoreType.REGULAR((4,)),
        ],
        compiler_params=pltpu.CompilerParams(
            collective_id=0, has_side_effects=True, vmem_limit_bytes=40 << 20
        ),
        name="couple",
    )(*(pltpu.with_memory_space_constraint(x, pltpu.HBM) for x in inputs))
    parts = 4
    results = (tracers, east, north, temp)
    tracers, east, north, temp = pl.pallas_call(
        store,
        out_shape=tuple(jax.ShapeDtypeStruct(x.shape, f32) for x in results),
        in_specs=[pl.BlockSpec(memory_space=pltpu.VMEM)] * 4,
        out_specs=[pl.BlockSpec(memory_space=pl.ANY)] * 4,
        scratch_shapes=[dma((parts + 3,))],
        compiler_params=pltpu.CompilerParams(vmem_limit_bytes=40 << 20),
        name="store",
    )(*(pltpu.with_memory_space_constraint(x, pltpu.VMEM) for x in results))
    return tracers.reshape(own_tr, levels, rows, width), east, north, temp


def solution(mesh):
    sizes = (mesh.shape["group"], mesh.shape["lat"], mesh.shape["lon"])
    fields = P("group", "lat", "lon")
    return jax.shard_map(
        functools.partial(local, sizes),
        mesh=mesh,
        in_specs=(
            P("group", None, "lat", "lon"),
            fields,
            fields,
            fields,
            fields,
            fields,
            P("lat", "lon"),
            P(),
            P(),
            P(),
        ),
        out_specs=(P("group", None, "lat", "lon"), fields, fields, fields),
        check_vma=False,
    )
```

```python
import functools

import jax
import jax.numpy as jnp
from jax import lax
from jax.experimental import pallas as pl
from jax.experimental.pallas import tpu as pltpu
from jax.sharding import PartitionSpec as P

MESH = pl.DeviceIdType.MESH
diffusion = 0.1
pressure = 0.05
chem_step = 0.2


def kernel(
    sizes,
    species,
    east,
    north,
    up,
    warm,
    dens,
    counts,
    comp,
    stoi,
    heat,
    tracers,
    east_out,
    north_out,
    temp_out,
    raw,
    cells,
    packs,
    edges,
    edges_in,
    fix,
    adv,
    block,
    reacted,
    back,
    own,
    winds,
    side_in,
    rim_out,
    rim_in,
    coef,
    misc,
    count_v,
    comp_v,
    stoi_v,
    heat_v,
    heat_b,
    load_sem,
    wind_sem,
    lat_sem,
    rim_sem,
    pack_sem,
    lon_sem,
    side_sem,
    fwd_sem,
    back_sem,
    ok_sem,
):
    groups, lats, lons = sizes
    g, la, lo = lax.axis_index("group"), lax.axis_index("lat"), lax.axis_index("lon")
    levels, rows, own_tr, width = adv.shape
    species_all = comp_v.shape[1]
    repeats = comp_v.shape[0] // species_all
    pieces = rows // 2
    peers = [lax.rem(g + k, groups) for k in range(1, groups)]
    far_first = sorted(range(groups - 1), key=lambda k: -min(k + 1, groups - 1 - k))
    has_s, has_n, has_w, has_e = la > 0, la < lats - 1, lo > 0, lo < lons - 1
    dev_s, dev_n, dev_w, dev_e = (g, la - 1, lo), (g, la + 1, lo), (g, la, lo - 1), (g, la, lo + 1)

    turned = la == 3 * lats // 4
    odd = lax.rem(lo, 2) == 1
    near = [
        (has_s, dev_s, turned),
        (has_n, dev_n, la != 3 * lats // 4 - 1),
        (has_w, dev_w, odd),
        (has_e, dev_e, odd),
    ]
    leads = [jnp.logical_and(has, lead) for has, _, lead in near]
    follows = [jnp.logical_and(has, jnp.logical_not(lead)) for has, _, lead in near]
    barrier = pltpu.get_barrier_semaphore()

    def greet(dev):
        pl.semaphore_signal(barrier, inc=1, device_id=dev, device_id_type=MESH)

    for p in peers:
        greet((p, la, lo))
    for lead, (_, dev, _) in zip(leads, near):
        pl.when(lead)(functools.partial(greet, dev))

    def answer(i):
        pl.semaphore_signal(
            ok_sem.at[i ^ 1], inc=1, device_id=near[i][1], device_id_type=MESH
        )

    def await_answer(i):
        pl.when(leads[i])(lambda: pl.semaphore_wait(ok_sem.at[i], 1))

    part = own_tr * levels * rows // 4
    loads = [
        pltpu.make_async_copy(src, dst, load_sem.at[i])
        for i, (src, dst) in enumerate(
            [
                (species.at[pl.ds(n * part, part)], raw.at[pl.ds(n * part, part)])
                for n in range(4)
            ]
            + [
                (up.at[0], own.at[0]),
                (east.at[0], own.at[1]),
                (north.at[0], own.at[2]),
                (warm.at[0], own.at[3]),
                (dens.at[0], misc.at[0]),
                (counts, count_v),
                (comp, comp_v),
                (stoi, stoi_v),
                (heat, heat_v),
            ]
        )
    ]
    for i in list(range(4, 8)) + list(range(4)) + list(range(8, 13)):
        loads[i].start()

    @pl.when(jnp.logical_not(has_s))
    def _():
        cells[:, 0] = jnp.zeros((levels, own_tr, width), jnp.float32)
        rim_in[0] = jnp.zeros((8, width), jnp.float32)

    @pl.when(jnp.logical_not(has_n))
    def _():
        cells[:, rows + 1] = jnp.zeros((levels, own_tr, width), jnp.float32)
        rim_in[1] = jnp.zeros((8, width), jnp.float32)

    @pl.when(jnp.logical_not(has_w))
    def _():
        edges_in[0] = jnp.zeros((groups, 8, width), jnp.float32)
        side_in[0] = jnp.zeros((3, rows, width), jnp.float32)

    @pl.when(jnp.logical_not(has_e))
    def _():
        edges_in[1] = jnp.zeros((groups, 8, width), jnp.float32)
        side_in[1] = jnp.zeros((3, rows, width), jnp.float32)

    for i in range(4, 7):
        loads[i].wait()
    pl.semaphore_wait(barrier, groups - 1 + sum(f.astype(jnp.int32) for f in follows))
    for i in range(4):
        pl.when(follows[i])(functools.partial(answer, i))

    def remote(src, dst, sems, index, dev):
        return pltpu.make_async_remote_copy(
            src_ref=src,
            dst_ref=dst,
            send_sem=sems.at[(0,) + index],
            recv_sem=sems.at[(1,) + index],
            device_id=dev,
            device_id_type=MESH,
        )

    def wind_copies(k, level):
        return [
            remote(own.at[f], winds.at[level, f], wind_sem, (f, k), (peers[k], la, lo))
            for f in range(3)
        ]

    for k in far_first:
        for copy in wind_copies(k, g):
            copy.start()

    lane = lax.broadcasted_iota(jnp.int32, (own_tr, width), 1)

    for i in (0, 1, 2, 3, 7):
        loads[i].wait()
    winds[g] = own[0:3]

    def turn(r, packed):
        done = []
        hit = jnp.logical_or(lane == 2 * r, lane == lax.rem(2 * r + width - 1, width))
        for l in range(levels):
            tile = raw[pl.ds(l * rows + r, own_tr, stride=levels * rows), :]
            cells[l, r + 1] = tile
            done.append(jnp.where(hit, pltpu.roll(tile, 2 * r, 1), packed[l]))
        return tuple(done)

    zero = jnp.zeros((own_tr, width), jnp.float32)
    folds = own_tr // 8
    share = width // folds
    lane8 = lax.broadcasted_iota(jnp.int32, (8, width), 1)
    holder = lax.rem(lane8 + 1, width) // share
    for l, packed in enumerate(lax.fori_loop(0, rows, turn, (zero,) * levels)):
        folded = packed[0:8]
        for n in range(1, folds):
            folded = jnp.where(
                holder == n, pltpu.roll(packed[8 * n : 8 * n + 8], share * n, 1), folded
            )
        packs[l] = folded

    mine = pl.ds(pl.multiple_of(g * own_tr, own_tr), own_tr)

    def part_of(group):
        return pl.ds(pl.multiple_of(group * own_tr, own_tr), own_tr)

    def pack_copy(k, group):
        return remote(
            packs.at[peers[k]], edges.at[group], pack_sem, (k,), (peers[k], la, lo)
        )

    for k in far_first:
        pack_copy(k, g).start()
    edges[g] = packs[g]
    lon_copies = [
        (has_e, has_w, remote(edges, edges_in.at[0], lon_sem, (0,), dev_e)),
        (has_w, has_e, remote(edges, edges_in.at[1], lon_sem, (1,), dev_w)),
    ]
    side_copies = [
        (has_e, has_w, remote(own.at[pl.ds(1, 3)], side_in.at[0], side_sem, (0,), dev_e)),
        (has_w, has_e, remote(own.at[pl.ds(1, 3)], side_in.at[1], side_sem, (1,), dev_w)),
    ]
    lat_copies = [
        (has_n, has_s, remote(cells.at[:, rows], cells.at[:, 0], lat_sem, (0,), dev_n)),
        (has_s, has_n, remote(cells.at[:, 1], cells.at[:, rows + 1], lat_sem, (1,), dev_s)),
    ]
    rim_copies = [
        (has_n, has_s, remote(rim_out.at[0], rim_in.at[0], rim_sem, (0,), dev_n)),
        (has_s, has_n, remote(rim_out.at[1], rim_in.at[1], rim_sem, (1,), dev_s)),
    ]

    def start_all(copies):
        for sends, _, copy in copies:
            pl.when(sends)(copy.start)

    def receive_all(copies):
        for _, receives, copy in copies:
            pl.when(receives)(copy.wait_recv)

    def start_lat(copies, which):
        pl.when(which[1])(copies[0][2].start)
        pl.when(which[0])(copies[1][2].start)

    start_lat(lat_copies, follows)

    for k in range(groups - 1):
        for copy in wind_copies(k, lax.rem(g + groups - 1 - k, groups)):
            copy.wait_recv()
    for l in range(levels):
        rim_out[0, l : l + 1, :] = winds[l, 2, rows - 1 : rows, :]
        rim_out[1, l : l + 1, :] = winds[l, 2, 0:1, :]
    for j in range(3):
        rim_out[0, levels + j : levels + j + 1, :] = own[1 + j, rows - 1 : rows, :]
        rim_out[1, levels + j : levels + j + 1, :] = own[1 + j, 0:1, :]
    start_lat(rim_copies, follows)

    row_at = lax.broadcasted_iota(jnp.int32, (rows, width), 0)
    lane_at = lax.broadcasted_iota(jnp.int32, (rows, width), 1)

    def from_west(f, edge):
        return jnp.where(lane_at == 0, pltpu.roll(edge, 1, 1), pltpu.roll(f, 1, 1))

    def from_east(f, edge):
        return jnp.where(
            lane_at == width - 1, pltpu.roll(edge, width - 1, 1), pltpu.roll(f, width - 1, 1)
        )

    def from_south(f, edge):
        return jnp.where(row_at == 0, edge, pltpu.roll(f, 1, 0))

    def from_north(f, edge):
        return jnp.where(row_at == rows - 1, edge, pltpu.roll(f, rows - 1, 0))

    def zonal_vertical():
        for l in range(levels):
            u = winds[l, 1]
            a_e = jnp.where(lane_at < width - 1, 0.5 * (u + pltpu.roll(u, width - 1, 1)), 0.0)
            a_w = jnp.where(lane_at > 0, 0.5 * (pltpu.roll(u, 1, 1) + u), 0.0)
            keep = 1.0 - jnp.maximum(a_e, 0.0) + jnp.minimum(a_w, 0.0)
            coef[1, l] = -jnp.minimum(a_e, 0.0)
            coef[2, l] = jnp.maximum(a_w, 0.0)
            if l < levels - 1:
                a_u = 0.5 * (winds[l, 0] + winds[l + 1, 0])
                keep = keep - jnp.maximum(a_u, 0.0)
                coef[5, l] = -jnp.minimum(a_u, 0.0)
            if l > 0:
                a_d = 0.5 * (winds[l - 1, 0] + winds[l, 0])
                keep = keep + jnp.minimum(a_d, 0.0)
                coef[6, l] = jnp.maximum(a_d, 0.0)
            coef[7, l] = keep

    def meridional(south_rim, north_rim):
        for l in range(levels):
            v = winds[l, 2]
            a_n = 0.5 * (v + from_north(v, north_rim(l)))
            a_s = 0.5 * (from_south(v, south_rim(l)) + v)
            coef[3, l] = -jnp.minimum(a_n, 0.0)
            coef[4, l] = jnp.maximum(a_s, 0.0)
            coef[0, l] = coef[7, l] - jnp.maximum(a_n, 0.0) + jnp.minimum(a_s, 0.0)

    zonal_vertical()
    meridional(lambda l: winds[l, 2, 0:1, :], lambda l: winds[l, 2, 0:1, :])
    def first_row(i):
        odd = i % 2
        half = i // 2
        middle = pieces // 2
        return 2 * (odd * (middle + half) + (1 - odd) * (middle - 1 - half))

    def forward_copy(i, k, part):
        r0 = first_row(i)
        part = part_of(part)
        return remote(
            adv.at[peers[k], pl.ds(r0, 2)],
            block.at[pl.ds(r0, 2), part],
            fwd_sem,
            (i, k),
            (peers[k], la, lo),
        )

    def advect(i, carry):
        r0 = first_row(i)
        for rr in range(2):
            r = r0 + rr
            for l in range(levels):

                def c(j):
                    return coef[j, l, pl.ds(r, 1), :]

                here = cells[l, r + 1]
                east_of = pltpu.roll(here, width - 1, 1)
                west_of = pltpu.roll(here, 1, 1)
                total = c(0) * here + c(1) * east_of + c(2) * west_of
                total = total + c(3) * cells[l, r + 2] + c(4) * cells[l, r]
                if l < levels - 1:
                    total = total + c(5) * cells[l + 1, r + 1]
                if l > 0:
                    total = total + c(6) * cells[l - 1, r + 1]
                adv[l, r] = total
            block[r, mine, :] = adv[g, r]
        for k in far_first:
            forward_copy(i, k, g).start()
        return carry

    lax.fori_loop(0, 2, advect, 0)

    for k in range(groups - 1):
        pack_copy(k, lax.rem(g + groups - 1 - k, groups)).wait_recv()
    await_answer(3)
    pl.when(has_e)(side_copies[0][2].start)
    pl.when(has_e)(lon_copies[0][2].start)
    await_answer(2)
    pl.when(has_w)(side_copies[1][2].start)
    pl.when(has_w)(lon_copies[1][2].start)

    lax.fori_loop(2, pieces - 2, advect, 0)

    await_answer(0)
    await_answer(1)
    start_lat(lat_copies, leads)
    start_lat(rim_copies, leads)
    for i in range(8, 13):
        loads[i].wait()
    t = own[3]
    misc[1] = 1.0 / (1.0 + jnp.exp(-2.0 * t))
    heat_b[...] = jnp.transpose(jnp.broadcast_to(heat_v[...], (species_all, species_all)))

    def back_copy(i, k, level):
        r0 = first_row(i)
        part = part_of(peers[k])
        return remote(
            reacted.at[pl.ds(r0, 2), part],
            back.at[level, pl.ds(r0, 2)],
            back_sem,
            (i, k),
            (peers[k], la, lo),
        )

    receive_all(side_copies)
    u = own[1]
    a_w = 0.5 * (from_west(u, side_in[0, 0]) + u)
    a_e = 0.5 * (u + from_east(u, side_in[1, 0]))
    a_w = jnp.where(lax.rem(lane_at, share) == 2 * row_at, a_w[:, 0:1], 0.0)
    a_e = jnp.where(lax.rem(lane_at + 1, share) == 2 * row_at, a_e[:, width - 1 :], 0.0)
    a = jnp.sum(a_w + a_e, axis=0, keepdims=True)
    receive_all(lon_copies)
    first_lane = lax.rem(lane8, 2) == 0
    more, less = jnp.maximum(a, 0.0), jnp.minimum(a, 0.0)
    for n in range(groups):
        beyond = jnp.where(
            first_lane, pltpu.roll(edges_in[0, n], 1, 1), pltpu.roll(edges_in[1, n], width - 1, 1)
        )
        here = edges[n]
        folded = jnp.where(
            first_lane, more * beyond + less * here, -(more * here + less * beyond)
        )
        for m in range(folds):
            at = n * own_tr + 8 * m
            fix[at : at + 8, :] = pltpu.roll(folded, (width - share * m) % width, 1)

    twice = (la + 1) * rows > 3 * lats * rows // 4

    def react(i, carry):
        r0 = first_row(i)
        for k in range(groups - 1):
            forward_copy(i, k, lax.rem(g + groups - 1 - k, groups)).wait_recv()

        def pair_of(ref):
            return jnp.concatenate([ref[pl.ds(r0, 1), :], ref[pl.ds(r0 + 1, 1), :]], axis=1)

        rate = pair_of(misc.at[1])
        count = pair_of(count_v)

        def substep(current, counter):
            narrow = current.astype(jnp.bfloat16)
            pair_terms = jnp.dot(comp_v[...], narrow, preferred_element_type=jnp.float32)
            quad = (
                (pair_terms.reshape(repeats, species_all, 2 * width) * current[None])
                .reshape(repeats * species_all, 2 * width)
                .astype(jnp.bfloat16)
            )
            made = jnp.dot(stoi_v[...], quad, preferred_element_type=jnp.float32)
            later = current + chem_step * (rate * made - current)
            return jnp.where(counter < count, later, current)

        def load(ref):
            return jnp.concatenate([ref[r0], ref[r0 + 1]], axis=1)

        at_edge = lax.broadcasted_iota(jnp.int32, (species_all, width), 1)
        at_edge = jnp.logical_or(at_edge == 0, at_edge == width - 1)
        for r in (r0, r0 + 1):
            moved = pltpu.roll(fix[...], lax.rem(width - 2 * r, width), 1)
            block[r] = block[r] + jnp.where(at_edge, moved, 0.0)

        def keep(value):
            reacted[r0] = value[:, :width]
            reacted[r0 + 1] = value[:, width:]

        keep(substep(load(block), 0))

        @pl.when(twice)
        def _():
            keep(substep(load(reacted), 1))

        for k in far_first:
            back_copy(i, k, g).start()
        for rr in range(2):
            r = r0 + rr
            gain = heat_b[...] * (reacted[r] - block[r])
            misc[3, pl.ds(r, 1), :] = jnp.sum(gain, axis=0, keepdims=True)
        return carry

    far = jnp.logical_or(jnp.logical_and(lax.rem(la, 4) == 3, has_n), jnp.logical_and(lax.rem(la, 4) == 0, has_s))
    early = jnp.where(far, 3, 0)
    lax.fori_loop(0, early, react, 0)

    receive_all(rim_copies)
    receive_all(lat_copies)
    meridional(lambda l: rim_in[0, l : l + 1, :], lambda l: rim_in[1, l : l + 1, :])
    lax.fori_loop(pieces - 2, pieces, advect, 0)

    lax.fori_loop(early, pieces, react, 0)


    def around(f, j, west_tile, east_tile):
        s, n = rim_in[0, levels + j : levels + j + 1, :], rim_in[1, levels + j : levels + j + 1, :]
        return from_east(f, east_tile), from_west(f, west_tile), from_north(f, n), from_south(f, s)

    t_e, t_w, t_n, t_s = around(t, 2, side_in[0, 2], side_in[1, 2])
    u = own[1]
    e, w, n, s = around(u, 0, side_in[0, 0], side_in[1, 0])
    east_out[0] = u + diffusion * (e + w + n + s - 4.0 * u) - pressure * (t_e - t_w)
    v = own[2]
    e, w, n, s = around(v, 1, side_in[0, 1], side_in[1, 1])
    north_out[0] = v + diffusion * (e + w + n + s - 4.0 * v) - pressure * (t_n - t_s)
    misc[2] = t + diffusion * (t_e + t_w + t_n + t_s - 4.0 * t)

    temp_out[0] = misc[2] + misc[3] / misc[0]

    for sends, _, copy in lon_copies + lat_copies + side_copies + rim_copies:
        pl.when(sends)(copy.wait_send)
    for k in range(groups - 1):
        for copy in wind_copies(k, g):
            copy.wait_send()
        pack_copy(k, g).wait_send()

    def collect(i, carry):
        r0 = first_row(i)
        for k in range(groups - 1):
            forward_copy(i, k, g).wait_send()
            back_copy(i, k, g).wait_send()
        for rr in range(2):
            back[g, r0 + rr] = reacted[r0 + rr, mine, :]
        for k in range(groups - 1):
            back_copy(i, k, lax.rem(g + groups - 1 - k, groups)).wait_recv()
        for rr in range(2):
            for l in range(levels):
                at = l * rows + r0 + rr
                tracers[pl.ds(at, own_tr, stride=levels * rows), :] = back[l, r0 + rr]
        return carry

    lax.fori_loop(0, pieces, collect, 0)


def store(tracers, east, north, temp, tracers_out, east_out, north_out, temp_out, sem):
    parts = sem.shape[0] - 3
    part = tracers.shape[0] // parts
    pairs = [(tracers.at[pl.ds(n * part, part)], tracers_out.at[pl.ds(n * part, part)]) for n in range(parts)]
    pairs += [(east, east_out), (north, north_out), (temp, temp_out)]
    copies = [pltpu.make_async_copy(src, dst, sem.at[i]) for i, (src, dst) in enumerate(pairs)]
    for copy in copies:
        copy.start()
    for copy in copies:
        copy.wait()


def local(sizes, species, east, north, up, warm, dens, counts, comp, stoi, heat):
    own_tr, levels, rows, width = species.shape
    all_tr, terms = stoi.shape
    groups = sizes[0]
    pieces = rows // 2
    f32 = jnp.float32
    dma = pltpu.SemaphoreType.DMA
    inputs = (
        species.reshape(own_tr * levels * rows, width),
        east,
        north,
        up,
        warm,
        dens,
        counts,
        comp,
        stoi,
        heat.reshape(1, all_tr),
    )
    tracers, east, north, temp = pl.pallas_call(
        functools.partial(kernel, sizes),
        out_shape=(pltpu.VMEM((own_tr * levels * rows, width), f32),)
        + (pltpu.VMEM((1, rows, width), f32),) * 3,
        in_specs=[pl.BlockSpec(memory_space=pltpu.HBM)] * 10,
        out_specs=[pl.BlockSpec(memory_space=pltpu.VMEM)] * 4,
        scratch_shapes=[
            pltpu.VMEM((own_tr * levels * rows, width), f32),
            pltpu.VMEM((levels, rows + 2, own_tr, width), f32),
            pltpu.VMEM((levels, 8, width), f32),
            pltpu.VMEM((groups, 8, width), f32),
            pltpu.VMEM((2, groups, 8, width), f32),
            pltpu.VMEM((all_tr, width), f32),
            pltpu.VMEM((levels, rows, own_tr, width), f32),
            pltpu.VMEM((rows, all_tr, width), f32),
            pltpu.VMEM((rows, all_tr, width), f32),
            pltpu.VMEM((levels, rows, own_tr, width), f32),
            pltpu.VMEM((4, rows, width), f32),
            pltpu.VMEM((levels, 3, rows, width), f32),
            pltpu.VMEM((2, 3, rows, width), f32),
            pltpu.VMEM((2, 8, width), f32),
            pltpu.VMEM((2, 8, width), f32),
            pltpu.VMEM((8, levels, rows, width), f32),
            pltpu.VMEM((4, rows, width), f32),
            pltpu.VMEM((rows, width), jnp.int32),
            pltpu.VMEM((terms, all_tr), jnp.bfloat16),
            pltpu.VMEM((all_tr, terms), jnp.bfloat16),
            pltpu.VMEM((1, all_tr), f32),
            pltpu.VMEM((all_tr, all_tr), f32),
            dma((13,)),
            dma((2, 3, groups - 1)),
            dma((2, 2)),
            dma((2, 2)),
            dma((2, groups - 1)),
            dma((2, 2)),
            dma((2, 2)),
            dma((2, pieces, groups - 1)),
            dma((2, pieces, groups - 1)),
            pltpu.SemaphoreType.REGULAR((4,)),
        ],
        compiler_params=pltpu.CompilerParams(
            collective_id=0, has_side_effects=True, vmem_limit_bytes=40 << 20
        ),
        name="couple",
    )(*(pltpu.with_memory_space_constraint(x, pltpu.HBM) for x in inputs))
    parts = 4
    results = (tracers, east, north, temp)
    tracers, east, north, temp = pl.pallas_call(
        store,
        out_shape=tuple(jax.ShapeDtypeStruct(x.shape, f32) for x in results),
        in_specs=[pl.BlockSpec(memory_space=pltpu.VMEM)] * 4,
        out_specs=[pl.BlockSpec(memory_space=pl.ANY)] * 4,
        scratch_shapes=[dma((parts + 3,))],
        compiler_params=pltpu.CompilerParams(vmem_limit_bytes=40 << 20),
        name="store",
    )(*(pltpu.with_memory_space_constraint(x, pltpu.VMEM) for x in results))
    return tracers.reshape(own_tr, levels, rows, width), east, north, temp


def solution(mesh):
    sizes = (mesh.shape["group"], mesh.shape["lat"], mesh.shape["lon"])
    fields = P("group", "lat", "lon")
    return jax.shard_map(
        functools.partial(local, sizes),
        mesh=mesh,
        in_specs=(
            P("group", None, "lat", "lon"),
            fields,
            fields,
            fields,
            fields,
            fields,
            P("lat", "lon"),
            P(),
            P(),
            P(),
        ),
        out_specs=(P("group", None, "lat", "lon"), fields, fields, fields),
        check_vma=False,
    )
```
